512 devices in a mesh: pts: 16 (over x, z_hi, core), ctr: 32 (over z_lo, y).
Axes of the slice: x: 4, y: 4, z: 16 (z_hi: 2, z_lo: 8; z = z_hi * 8 + z_lo), core: 2. Of those that a mesh axis runs over, the one named last changes fastest.
Arguments:
- points: float32 [8192, 256], P('pts'), may hold values from -6 to 6
- labels: bfloat16 [8192, 256], P('pts'), may hold values from -6 to 6
- centres: float32 [2, 4096, 256], P(None, 'ctr'), may hold values from -6 to 6
- coeffs: float32 [2, 4096, 256], P(None, 'pts'), may hold values from -6 to 6
- diag_inverse: float32 [2, 4096, 4096], P(None, 'ctr', 'pts'), may hold values from -0.09375 to 0.09375
- off_block: float32 [4096, 4096], P('pts', 'ctr'), may hold values from -0.09375 to 0.09375
Outputs:
- transposed: float32 [2, 4096, 256], P(None, 'ctr', 'pts')
The draws below stay inside these ranges and needn't reach their ends.
All inputs are finite; a program needn't handle non-finite values.
Results may differ from the reference program's by a relative error of at most 0.0003.
Values sent between devices are 32-bit elements; how exact they have to be, the bound alone decides.
No kernel may reach another device: no remote copies, remote signals or barrier semaphores. Data moves between devices by JAX's collectives and lax.ppermute only.
A program may use at most 64 MiB of HBM per device.

```python
import math
import jax
import jax.numpy as jnp
from jax import lax

D = 256
R = 256
HALF = 4096
PANELS = 2
PTS_DEV = 512
N = 8192
N_PTS = 16


def raised(array, own_key, source, target, blocks, factor):
    def block_of(position):
        return (jnp.arange(array.shape[position]) // (array.shape[position] // blocks)).reshape((-1,) + (1,) * (array.ndim - 1 - position))

    one_side = jax.random.permutation(own_key, blocks)[block_of(target)]
    second = (block_of(target) + blocks // 2) % blocks
    return jnp.where((block_of(source) == one_side) | (block_of(source) == second), factor * array, array)


def shard_levels(key, shape, cuts, low, high):
    def one(axis_at, shards_of):
        heights = jax.random.uniform(jax.random.fold_in(jax.random.fold_in(key, 6), axis_at), (shards_of,), jnp.float32, low / len(cuts), high / len(cuts))
        return jnp.repeat(jnp.exp(heights), shape[axis_at] // shards_of).reshape((-1,) + (1,) * (len(shape) - axis_at - 1))

    level = one(*cuts[0])
    for cut in cuts[1:]:
        level = level * one(*cut)
    return level


def gaussian(rng, extent, deviation, most, cuts=(), dtype=jnp.bfloat16):
    drawn = jax.random.normal(rng, extent, jnp.float32) * deviation
    if len(cuts) > 0:
        drawn = shard_levels(rng, extent, cuts, -0.22, 0.18) * drawn
    return jnp.clip(drawn, min=-most, max=most).astype(dtype)


def bell_draw_with(key, dims, deviation, bound, split, heavy, dtype=jnp.bfloat16):
    array = deviation * jax.random.normal(key, dims, jnp.float32)
    if split:
        array = array * shard_levels(key, dims, split, -0.22, 0.18)
    return jnp.clip(raised(array, jax.random.fold_in(key, 3), *heavy), -bound, bound).astype(dtype)


def setup_inputs(seed: int = 0) -> dict:
    key_list = jax.random.split(jax.random.key(seed), 7)
    points = gaussian(key_list[0], (N, D), 1.0, 6.0, ((0, 16),), jnp.float32)
    labels = bell_draw_with(key_list[1], (N, R), 1.0, 6.0, ((0, 16),), (0, 1, 16, 2.0))
    centres = gaussian(key_list[2], (PANELS, HALF, D), 1.0, 6.0, ((1, 32),), jnp.float32)
    coeffs = gaussian(key_list[3], (PANELS, HALF, R), 1.0, 6.0, ((1, 16),), jnp.float32)
    diag_inverse = gaussian(key_list[4], (PANELS, HALF, HALF), HALF ** -0.5, 0.09375, ((1, 32), (2, 16)), jnp.float32)
    off_block = gaussian(key_list[5], (HALF, HALF), HALF ** -0.5, 0.09375, ((0, 16), (1, 32)), jnp.float32)
    return {"points": points, "labels": labels, "centres": centres, "coeffs": coeffs, "diag_inverse": diag_inverse, "off_block": off_block}


def reference(points, labels, centres, coeffs, diag_inverse, off_block):
    high = lax.Precision.HIGHEST
    second = jnp.dot(diag_inverse[1], coeffs[1], precision=high, preferred_element_type=jnp.float32)
    rest = coeffs[0] - jnp.dot(off_block, second, precision=high, preferred_element_type=jnp.float32)
    first = jnp.dot(diag_inverse[0], rest, precision=high, preferred_element_type=jnp.float32)
    solved = jnp.concatenate([first, second], axis=0)
    flat_centres = centres.reshape(PANELS * HALF, D)
    point_blocks = points.reshape(N_PTS, PTS_DEV, D)
    label_blocks = labels.reshape(N_PTS, PTS_DEV, R)
    pred_scale = 1.0 / (2.0 * math.sqrt(PANELS * HALF))

    def one_block(total, pair):
        block_points, block_labels = pair
        score = jnp.dot(block_points, flat_centres.T, precision=high, preferred_element_type=jnp.float32) / math.sqrt(D)
        kernel = score + score * score * score / 3.0
        pred = jnp.dot(kernel, solved, precision=high, preferred_element_type=jnp.float32) * pred_scale
        weights = jnp.tanh(pred - block_labels.astype(jnp.float32))
        return (total + jnp.dot(kernel.T, weights, precision=high, preferred_element_type=jnp.float32), None)
    start = jnp.zeros((PANELS * HALF, R), jnp.float32)
    total, unused = lax.scan(one_block, start, (point_blocks, label_blocks))
    total = total / (2.0 * math.sqrt(PTS_DEV * N_PTS))
    return total.reshape(PANELS, HALF, R)
```

```python
import math

import jax
import jax.numpy as jnp
from jax import lax
from jax.sharding import Mesh
from jax.sharding import PartitionSpec as P

PTS = ("x", "h", "c")
CTR = ("w", "z", "y")
SIZES = {"x": 4, "h": 2, "c": 2, "w": 2, "z": 4, "y": 4}
HIGH = lax.Precision.HIGH


def dot(a, b, ca, cb):
    return lax.dot_general(
        a, b, ((ca, cb), ((), ())), precision=HIGH, preferred_element_type=jnp.float32
    )


def swap_sum(a, axis):
    return a + lax.ppermute(a, axis, [(0, 1), (1, 0)])


def shot(a, axes):
    return lax.all_to_all(a, axes, 0, 0, tiled=True)


def spread(a, axes, n):
    return shot(jnp.broadcast_to(a[None], (n, *a.shape)), axes)


def sum_ctr(a):
    a = jnp.sum(spread(a, "z", 4), 0)
    return swap_sum(a, "w")


def column_block(a, rows):
    a = a.reshape(4, 2, 2, 4, 4, rows)
    a = lax.dynamic_index_in_dim(a, lax.axis_index("y"), 3, keepdims=False)
    return a.transpose(0, 2, 1, 3, 4).reshape(64, rows)


def local(points, labels, centres, coeffs, diag_inverse, off_block):
    part = dot(coeffs[1], diag_inverse[1], (0,), (1,))
    part = part.reshape(4, 2, 2, 16, 128).transpose(0, 2, 1, 3, 4).reshape(8, 32, 128)
    part = jnp.sum(shot(part, ("x", "c")), 0)
    part = swap_sum(part, "h")
    part = part.reshape(2, 4, 4, 128).transpose(1, 0, 2, 3).reshape(1, 4, 8, 128)
    part = jnp.broadcast_to(part, (8, 4, 8, 128)).reshape(32, 8, 128)
    second = shot(part, ("x", "c", "y"))
    second = second.reshape(8, 4, 8, 128).transpose(0, 2, 1, 3).reshape(64, 512)

    off_y = lax.all_gather(off_block, "y", axis=1, tiled=True)
    diag_y = lax.all_gather(diag_inverse[0], "y", axis=0, tiled=True)
    centres_y = lax.all_gather(centres, "y", axis=0)

    carried = sum_ctr(dot(second, off_y, (1,), (1,)))
    rest = column_block(coeffs[0].T, 256) - carried
    first = dot(rest, diag_y, (1,), (1,))
    first = jnp.sum(shot(first.reshape(8, 8, 512), ("x", "c")), 0)
    first = swap_sum(first, "h")
    first = spread(first, ("x", "c"), 8).reshape(64, 512)

    def kernel_tile(panel):
        flat = centres_y[:, panel].reshape(512, 256)
        score = dot(points, flat, (1,), (1,)) / math.sqrt(points.shape[1])
        return score + score * score * score / 3.0

    kernel0, kernel1 = kernel_tile(0), kernel_tile(1)
    total_centres = 2 * 512 * 8
    pred_scale = 1.0 / (2.0 * math.sqrt(total_centres))
    pred = dot(first, kernel0, (1,), (1,)) + dot(second, kernel1, (1,), (1,))
    pred = sum_ctr(pred)
    target = column_block(labels.astype(jnp.float32).T, 512)
    weights = jnp.tanh(pred * pred_scale - target)

    total_points = points.shape[0] * 16
    scale = 1.0 / (2.0 * math.sqrt(total_points))
    term0 = dot(weights, kernel0, (1,), (0,)).reshape(8, 8, 4, 128)
    term1 = dot(weights, kernel1, (1,), (0,)).reshape(8, 8, 4, 128)
    term = jnp.stack([term0, term1], 3)
    term = term.transpose(0, 2, 1, 3, 4).reshape(32, 8, 256)
    term = jnp.sum(shot(term, ("x", "c", "y")).reshape(8, 4, 8, 256), 0)
    term = term.reshape(4, 2, 4, 256).transpose(1, 0, 2, 3).reshape(2, 16, 256)
    h = lax.axis_index("h")
    mine = lax.dynamic_index_in_dim(term, h, 0, keepdims=False)
    other = lax.dynamic_index_in_dim(term, 1 - h, 0, keepdims=False)
    mine = (mine + lax.ppermute(other, "h", [(0, 1), (1, 0)])) * scale
    return mine.reshape(16, 2, 128).transpose(1, 2, 0)


def solution(mesh):
    fine = Mesh(mesh.devices.reshape(tuple(SIZES.values())), tuple(SIZES))
    return jax.shard_map(
        local,
        mesh=fine,
        in_specs=(
            P(PTS, None),
            P(PTS, None),
            P(None, CTR, None),
            P(None, PTS, None),
            P(None, CTR, PTS),
            P(PTS, CTR),
        ),
        out_specs=P(None, CTR, PTS),
        check_vma=False,
    )
```

```python
import math

import jax
import jax.numpy as jnp
from jax import lax
from jax.sharding import Mesh
from jax.sharding import PartitionSpec as P

PTS = ("x", "h", "c")
CTR = ("w", "z", "y")
SIZES = {"x": 4, "h": 2, "c": 2, "w": 2, "z": 4, "y": 4}
HIGH = lax.Precision.HIGH


def dot(a, b, ca, cb):
    return lax.dot_general(
        a, b, ((ca, cb), ((), ())), precision=HIGH, preferred_element_type=jnp.float32
    )


def swap_sum(a, axis):
    return a + lax.ppermute(a, axis, [(0, 1), (1, 0)])


def shot(a, axes):
    return lax.all_to_all(a, axes, 0, 0, tiled=True)


def spread(a, axes, n):
    return shot(jnp.broadcast_to(a[None], (n, *a.shape)), axes)


def pick(first, count):
    row = lax.broadcasted_iota(jnp.int32, (count, 256), 0) + first
    column = lax.broadcasted_iota(jnp.int32, (count, 256), 1)
    x, c, h, t = row // 16, row // 8 % 2, row // 4 % 2, row % 4
    return column == ((x * 2 + h) * 2 + c) * 16 + lax.axis_index("y") * 4 + t


def local(points, labels, centres, coeffs, diag_inverse, off_block):
    part = dot(coeffs[1], diag_inverse[1], (0,), (1,))
    part = part.reshape(4, 2, 2, 16, 128).transpose(0, 2, 1, 3, 4).reshape(8, 32, 128)
    part = jnp.sum(shot(part, ("x", "c")), 0)

    off_wide = off_block.reshape(2, 128, 128).transpose(1, 0, 2).reshape(128, 256)
    own = jnp.concatenate([off_wide, diag_inverse[0], centres.reshape(256, 256)], 0)
    part, own = lax.optimization_barrier((part, own))
    blocks = spread(own, "y", 4)
    off_y = blocks[:, :128].reshape(4, 128, 2, 128).transpose(2, 1, 0, 3).reshape(256, 512)
    diag_y = blocks[:, 128:256].reshape(512, 256)

    part = swap_sum(part, "h")
    part = part.reshape(2, 4, 4, 128).transpose(1, 0, 2, 3).reshape(1, 4, 8, 128)
    part = jnp.broadcast_to(part, (8, 4, 8, 128)).reshape(32, 8, 128)
    second = shot(part, ("x", "c", "y"))
    second = second.reshape(8, 4, 8, 128).transpose(0, 2, 1, 3).reshape(64, 512)

    carried = dot(second, off_y, (1,), (1,))
    carried = jnp.sum(spread(carried, "z", 4), 0)
    carried = swap_sum(carried, "w")
    chosen = pick(0, 64).astype(jnp.float32)
    rest = lax.dot_general(
        chosen,
        coeffs[0],
        (((1,), (1,)), ((), ())),
        precision=lax.Precision.HIGHEST,
        preferred_element_type=jnp.float32,
    )
    first = dot(rest - carried, diag_y, (1,), (1,))
    first = swap_sum(first, "c")
    first = jnp.sum(spread(first, "x", 4), 0)
    first = swap_sum(first, "h")

    def kernel_tile(panel):
        flat = blocks[:, 256 + 128 * panel : 384 + 128 * panel].reshape(512, 256)
        score = dot(points, flat, (1,), (1,)) / math.sqrt(points.shape[1])
        return score + score * score * score / 3.0

    kernel0, kernel1 = kernel_tile(0), kernel_tile(1)
    total_centres = 2 * 512 * 8
    pred_scale = 1.0 / (2.0 * math.sqrt(total_centres))
    pred = dot(first, kernel0, (1,), (1,)) + dot(second, kernel1, (1,), (1,))
    pred = jnp.sum(shot(pred.reshape(4, 16, 512), "z"), 0)
    pred = swap_sum(pred, "w")
    quarter = pick(lax.axis_index("z") * 16, 16).astype(labels.dtype)
    target = lax.dot_general(
        quarter, labels, (((1,), (1,)), ((), ())), preferred_element_type=jnp.float32
    )
    weights = jnp.tanh(pred * pred_scale - target)
    weights = spread(weights, "z", 4).reshape(64, 512)

    total_points = points.shape[0] * 16
    scale = 1.0 / (2.0 * math.sqrt(total_points))
    term0 = dot(weights, kernel0, (1,), (0,)).reshape(8, 8, 4, 128)
    term1 = dot(weights, kernel1, (1,), (0,)).reshape(8, 8, 4, 128)
    term = jnp.stack([term0, term1], 3)
    term = term.transpose(0, 2, 1, 3, 4).reshape(32, 8, 256)
    term = jnp.sum(shot(term, ("x", "c", "y")).reshape(8, 4, 8, 256), 0)
    term = term.reshape(4, 2, 4, 256).transpose(1, 0, 2, 3).reshape(2, 16, 256)
    h = lax.axis_index("h")
    mine = lax.dynamic_index_in_dim(term, h, 0, keepdims=False)
    other = lax.dynamic_index_in_dim(term, 1 - h, 0, keepdims=False)
    mine = (mine + lax.ppermute(other, "h", [(0, 1), (1, 0)])) * scale
    return mine.reshape(16, 2, 128).transpose(1, 2, 0)


def solution(mesh):
    fine = Mesh(mesh.devices.reshape(tuple(SIZES.values())), tuple(SIZES))
    return jax.shard_map(
        local,
        mesh=fine,
        in_specs=(
            P(PTS, None),
            P(PTS, None),
            P(None, CTR, None),
            P(None, PTS, None),
            P(None, CTR, PTS),
            P(PTS, CTR),
        ),
        out_specs=P(None, CTR, PTS),
        check_vma=False,
    )
```

```python
import math

import jax
import jax.numpy as jnp
from jax import lax
from jax.sharding import Mesh
from jax.sharding import PartitionSpec as P

PTS = ("x", "h", "c")
CTR = ("w", "z", "y")
SIZES = {"x": 4, "h": 2, "c": 2, "w": 2, "z": 4, "y": 4}
HIGH = lax.Precision.HIGH


def dot(a, b, ca, cb):
    return lax.dot_general(
        a, b, ((ca, cb), ((), ())), precision=HIGH, preferred_element_type=jnp.float32
    )


def swap_sum(a, axis):
    return a + lax.ppermute(a, axis, [(0, 1), (1, 0)])


def shot(a, axes):
    return lax.all_to_all(a, axes, 0, 0, tiled=True)


def spread(a, axes, n):
    return shot(jnp.broadcast_to(a[None], (n, *a.shape)), axes)


def pick(first, count):
    row = lax.broadcasted_iota(jnp.int32, (count, 256), 0) + first
    column = lax.broadcasted_iota(jnp.int32, (count, 256), 1)
    x, c, h, t = row // 16, row // 8 % 2, row // 4 % 2, row % 4
    return column == ((x * 2 + h) * 2 + c) * 16 + lax.axis_index("y") * 4 + t


def local(points, labels, centres, coeffs, diag_inverse, off_block):
    part = dot(coeffs[1], diag_inverse[1], (0,), (1,))
    part = part.reshape(4, 2, 2, 16, 128).transpose(0, 2, 1, 3, 4).reshape(8, 32, 128)
    part = jnp.sum(shot(part, ("x", "c")), 0)

    part, off_block = lax.optimization_barrier((part, off_block))
    off_y = spread(off_block, "y", 4)
    part = swap_sum(part, "h")
    part, off_y = lax.optimization_barrier((part, off_y))
    off_y = off_y.transpose(1, 0, 2).reshape(256, 512)
    part = part.reshape(2, 4, 4, 128).transpose(1, 0, 2, 3).reshape(1, 4, 8, 128)
    part = jnp.broadcast_to(part, (8, 4, 8, 128)).reshape(32, 8, 128)
    second = shot(part, ("x", "c", "y"))
    second = second.reshape(8, 4, 8, 128).transpose(0, 2, 1, 3).reshape(64, 512)

    carried = dot(second, off_y, (1,), (1,))
    carried = jnp.sum(spread(carried, "z", 4), 0)
    carried, diag = lax.optimization_barrier((carried, diag_inverse[0]))
    diag_y = spread(diag, "y", 4).reshape(512, 256)
    carried = swap_sum(carried, "w")
    chosen = pick(0, 64).astype(jnp.float32)
    rest = lax.dot_general(
        chosen,
        coeffs[0],
        (((1,), (1,)), ((), ())),
        precision=lax.Precision.HIGHEST,
        preferred_element_type=jnp.float32,
    )
    first = dot(rest - carried, diag_y, (1,), (1,))
    first = jnp.sum(shot(first.reshape(8, 8, 512), ("x", "c")), 0)
    first, centres = lax.optimization_barrier((first, centres))
    centres_y = spread(centres.reshape(256, 256), "y", 4).reshape(4, 2, 128, 256)
    first = swap_sum(first, "h")
    first, centres_y = lax.optimization_barrier((first, centres_y))
    first = spread(first, ("x", "c"), 8).reshape(64, 512)

    def kernel_tile(panel):
        flat = centres_y[:, panel].reshape(512, 256)
        score = dot(points, flat, (1,), (1,)) / math.sqrt(points.shape[1])
        return score + score * score * score / 3.0

    kernel0, kernel1 = kernel_tile(0), kernel_tile(1)
    total_centres = 2 * 512 * 8
    pred_scale = 1.0 / (2.0 * math.sqrt(total_centres))
    pred = dot(first, kernel0, (1,), (1,)) + dot(second, kernel1, (1,), (1,))
    pred = jnp.sum(shot(pred.reshape(4, 16, 512), "z"), 0)
    pred = swap_sum(pred, "w")
    quarter = pick(lax.axis_index("z") * 16, 16).astype(labels.dtype)
    target = lax.dot_general(
        quarter, labels, (((1,), (1,)), ((), ())), preferred_element_type=jnp.float32
    )
    weights = jnp.tanh(pred * pred_scale - target)
    weights = spread(weights, "z", 4).reshape(64, 512)

    total_points = points.shape[0] * 16
    scale = 1.0 / (2.0 * math.sqrt(total_points))
    term0 = dot(weights, kernel0, (1,), (0,)).reshape(8, 8, 4, 128)
    term1 = dot(weights, kernel1, (1,), (0,)).reshape(8, 8, 4, 128)
    term = jnp.stack([term0, term1], 3)
    term = term.transpose(0, 2, 1, 3, 4).reshape(32, 8, 256)
    term = jnp.sum(shot(term, ("x", "c", "y")).reshape(8, 4, 8, 256), 0)
    term = term.reshape(4, 2, 4, 256).transpose(1, 0, 2, 3).reshape(2, 16, 256)
    h = lax.axis_index("h")
    mine = lax.dynamic_index_in_dim(term, h, 0, keepdims=False)
    other = lax.dynamic_index_in_dim(term, 1 - h, 0, keepdims=False)
    mine = (mine + lax.ppermute(other, "h", [(0, 1), (1, 0)])) * scale
    return mine.reshape(16, 2, 128).transpose(1, 2, 0)


def solution(mesh):
    fine = Mesh(mesh.devices.reshape(tuple(SIZES.values())), tuple(SIZES))
    return jax.shard_map(
        local,
        mesh=fine,
        in_specs=(
            P(PTS, None),
            P(PTS, None),
            P(None, CTR, None),
            P(None, PTS, None),
            P(None, CTR, PTS),
            P(PTS, CTR),
        ),
        out_specs=P(None, CTR, PTS),
        check_vma=False,
    )
```

```python
import math

import jax
import jax.numpy as jnp
from jax import lax
from jax.sharding import Mesh
from jax.sharding import PartitionSpec as P

PTS = ("x", "h", "c")
CTR = ("w", "z", "y")
SIZES = {"x": 4, "h": 2, "c": 2, "w": 2, "z": 4, "y": 4}
HIGH = lax.Precision.HIGH


def dot(a, b, ca, cb):
    return lax.dot_general(
        a, b, (((ca,), (cb,)), ((), ())), precision=HIGH, preferred_element_type=jnp.float32
    )


def swap(a, axis):
    return lax.ppermute(a, axis, [(0, 1), (1, 0)])


def scatter_sum(a, axes, n):
    a = a.reshape(n, a.shape[0] // n, a.shape[1])
    return jnp.sum(lax.all_to_all(a, axes, 0, 0, tiled=True), 0)


def gather(a, axes, n):
    a = jnp.broadcast_to(a[None], (n, *a.shape))
    return lax.all_to_all(a, axes, 0, 0, tiled=True).reshape(-1, a.shape[2])


def sum_pts(a):
    a = scatter_sum(a, ("x", "c"), 8)
    a = a + swap(a, "h")
    return gather(a, ("x", "c"), 8)


def columns(a):
    rows = a.shape[0]
    return a.reshape(rows, 4, 2, 2, 16).transpose(1, 3, 2, 4, 0).reshape(256, rows)


def local(points, labels, centres, coeffs, diag_inverse, off_block):
    second = sum_pts(dot(columns(coeffs[1]), diag_inverse[1], 1, 1))

    carried = dot(second, off_block, 1, 1)
    carried = scatter_sum(carried, ("z", "y"), 16)
    carried = carried + swap(carried, "w")
    carried = gather(carried, ("z", "y"), 16)

    first = sum_pts(dot(columns(coeffs[0]) - carried, diag_inverse[0], 1, 1))

    solved = jnp.concatenate([first, second], 1)
    score = dot(points, centres.reshape(256, 256), 1, 1) / math.sqrt(points.shape[1])
    kernel = score + score * score * score / 3.0
    pred_scale = 1.0 / (2.0 * math.sqrt(256 * 32))
    pred = scatter_sum(dot(solved, kernel, 1, 1), ("z", "y"), 16)
    pred = pred + swap(pred, "w")

    block = lax.axis_index("z") * 4 + lax.axis_index("y")
    x, c, h = block // 4, block // 2 % 2, block % 2
    start = ((x * 2 + h) * 2 + c) * 16
    row = lax.broadcasted_iota(jnp.int32, (16, 256), 0)
    chosen = lax.broadcasted_iota(jnp.int32, (16, 256), 1) == row + start
    target = lax.dot_general(
        chosen.astype(labels.dtype),
        labels,
        (((1,), (1,)), ((), ())),
        preferred_element_type=jnp.float32,
    )
    weights = gather(jnp.tanh(pred * pred_scale - target), ("z", "y"), 16)

    scale = 1.0 / (2.0 * math.sqrt(points.shape[0] * 16))
    term = scatter_sum(dot(weights, kernel, 1, 0), ("x", "c"), 8).reshape(2, 16, 256)
    h = lax.axis_index("h")
    mine = lax.dynamic_index_in_dim(term, h, 0, keepdims=False)
    other = lax.dynamic_index_in_dim(term, 1 - h, 0, keepdims=False)
    mine = (mine + swap(other, "h")) * scale
    return mine.reshape(16, 2, 128).transpose(1, 2, 0)


def solution(mesh):
    fine = Mesh(mesh.devices.reshape(tuple(SIZES.values())), tuple(SIZES))
    return jax.shard_map(
        local,
        mesh=fine,
        in_specs=(
            P(PTS, None),
            P(PTS, None),
            P(None, CTR, None),
            P(None, PTS, None),
            P(None, CTR, PTS),
            P(PTS, CTR),
        ),
        out_specs=P(None, CTR, PTS),
        check_vma=False,
    )
```

```python
import math

import jax
import jax.numpy as jnp
from jax import lax
from jax.sharding import Mesh
from jax.sharding import PartitionSpec as P

PTS = ("x", "h", "c")
CTR = ("w", "z", "y")
SIZES = {"x": 4, "h": 2, "c": 2, "w": 2, "z": 4, "y": 4}
HIGH = lax.Precision.HIGH


def dot(a, b, ca, cb):
    return lax.dot_general(
        a, b, (((ca,), (cb,)), ((), ())), precision=HIGH, preferred_element_type=jnp.float32
    )


def swap(a, axis):
    return lax.ppermute(a, axis, [(0, 1), (1, 0)])


def scatter_sum(a, axes):
    return jnp.sum(lax.all_to_all(a, axes, 0, 0, tiled=True), 0)


def gather(a, axes, n):
    a = jnp.broadcast_to(a[None], (n, *a.shape))
    return lax.all_to_all(a, axes, 0, 0, tiled=True)


def columns(a):
    rows = a.shape[0]
    return a.reshape(rows, 4, 2, 2, 16).transpose(1, 3, 2, 4, 0).reshape(256, rows)


def local(points, labels, centres, coeffs, diag_inverse, off_block):
    xc, zy = ("x", "c"), ("z", "y")
    off_all = lax.all_gather(off_block, xc, axis=0, tiled=True)

    part = jnp.concatenate(
        [
            dot(columns(coeffs[1]), diag_inverse[1], 1, 1),
            dot(columns(coeffs[0]), diag_inverse[0], 1, 1),
        ],
        1,
    )
    part = scatter_sum(part.reshape(8, 32, 256), xc)

    block = lax.axis_index("z") * 4 + lax.axis_index("y")
    label_rows = lax.dynamic_slice_in_dim(labels, block * 32, 32, 0).astype(jnp.float32)
    own = jnp.concatenate([diag_inverse[0], label_rows], 0)
    part, own = lax.optimization_barrier((part, own))
    both = lax.all_gather(own, xc, axis=0)
    diag_all = both[:, :128].reshape(8, 128, 2, 128).transpose(0, 2, 1, 3).reshape(16, 128, 128)
    label_all = both[:, 128:].reshape(256, 256)

    part = part + swap(part, "h")
    part, points = lax.optimization_barrier((part, points))
    points_all = lax.all_gather(points, xc, axis=0)
    second, direct = part[:, :128], part[:, 128:]

    carried = dot(second, off_all.reshape(16, 128, 128), 1, 2).transpose(1, 0, 2)
    carried = scatter_sum(carried, zy)
    carried = carried + swap(carried, "w")
    carried = gather(carried, zy, 16)
    carried = lax.dot_general(
        carried,
        diag_all,
        (((0, 2), (0, 2)), ((), ())),
        precision=HIGH,
        preferred_element_type=jnp.float32,
    )
    first = direct - (carried + swap(carried, "h"))

    solved = jnp.concatenate([first, second], 1)
    points_all = points_all.reshape(8, 16, 32, 256).transpose(1, 0, 2, 3).reshape(4096, 256)
    score = dot(points_all, centres.reshape(256, 256), 1, 1) / math.sqrt(points.shape[1])
    kernel = (score + score * score * score / 3.0).reshape(16, 256, 256)
    pred_scale = 1.0 / (2.0 * math.sqrt(256 * 32))
    pred = dot(solved, kernel, 1, 2).transpose(1, 0, 2)
    pred = scatter_sum(pred, zy)
    pred = pred + swap(pred, "w")

    x, c, h = lax.axis_index("x"), lax.axis_index("c"), lax.axis_index("h")
    row = lax.broadcasted_iota(jnp.int32, (32, 256), 0)
    start = ((x * 2 + row // 16) * 2 + c) * 16 + row % 16
    chosen = lax.broadcasted_iota(jnp.int32, (32, 256), 1) == start
    target = lax.dot_general(
        chosen.astype(jnp.float32),
        label_all,
        (((1,), (1,)), ((), ())),
        precision=lax.Precision.HIGHEST,
        preferred_element_type=jnp.float32,
    )
    weights = gather(jnp.tanh(pred * pred_scale - target), zy, 16)

    scale = 1.0 / (2.0 * math.sqrt(points.shape[0] * 16))
    term = lax.dot_general(
        weights,
        kernel,
        (((0, 2), (0, 1)), ((), ())),
        precision=HIGH,
        preferred_element_type=jnp.float32,
    ).reshape(2, 16, 256)
    mine = lax.dynamic_index_in_dim(term, h, 0, keepdims=False)
    other = lax.dynamic_index_in_dim(term, 1 - h, 0, keepdims=False)
    mine = (mine + swap(other, "h")) * scale
    return mine.reshape(16, 2, 128).transpose(1, 2, 0)


def solution(mesh):
    fine = Mesh(mesh.devices.reshape(tuple(SIZES.values())), tuple(SIZES))
    return jax.shard_map(
        local,
        mesh=fine,
        in_specs=(
            P(PTS, None),
            P(PTS, None),
            P(None, CTR, None),
            P(None, PTS, None),
            P(None, CTR, PTS),
            P(PTS, CTR),
        ),
        out_specs=P(None, CTR, PTS),
        check_vma=False,
    )
```

```python
import math

import jax
import jax.numpy as jnp
from jax import lax
from jax.sharding import Mesh
from jax.sharding import PartitionSpec as P

PTS = ("u", "v", "h", "c")
CTR = ("w", "z", "y")
SIZES = {"u": 2, "v": 2, "h": 2, "c": 2, "w": 2, "z": 4, "y": 4}
HIGH = lax.Precision.HIGH


def dot(a, b, ca, cb):
    return lax.dot_general(
        a, b, (((ca,), (cb,)), ((), ())), precision=HIGH, preferred_element_type=jnp.float32
    )


def swap(a, axis):
    return lax.ppermute(a, axis, [(0, 1), (1, 0)])


def scatter_sum(a, axes):
    return jnp.sum(lax.all_to_all(a, axes, 0, 0, tiled=True), 0)


def gather(a, axes, n):
    a = jnp.broadcast_to(a[None], (n, *a.shape))
    return lax.all_to_all(a, axes, 0, 0, tiled=True)


def columns(a):
    rows = a.shape[0]
    return a.reshape(rows, 4, 2, 2, 16).transpose(1, 3, 2, 4, 0).reshape(256, rows)


def local(points, labels, centres, coeffs, diag_inverse, off_block):
    xc, zy = ("u", "v", "c"), ("z", "y")
    h = lax.axis_index("h")
    block = lax.axis_index("z") * 4 + lax.axis_index("y")

    row = lax.broadcasted_iota(jnp.int32, (16, 256), 0)
    side = jnp.where(row < 8, h, 1 - h)
    start = block // 4 * 64 + side * 32 + block // 2 % 2 * 16 + block % 2 * 8 + row % 8
    chosen = (lax.broadcasted_iota(jnp.int32, (16, 256), 1) == start).astype(jnp.float32)

    def pick(a):
        return lax.dot_general(
            chosen,
            a.astype(jnp.float32),
            (((1,), (1,)), ((), ())),
            precision=lax.Precision.HIGHEST,
            preferred_element_type=jnp.float32,
        )

    label_chunk = pick(labels)
    coeff_chunk = pick(coeffs[0])
    point_slice = lax.dynamic_slice_in_dim(points, block * 32, 32, 0)
    pack = jnp.concatenate(
        [
            diag_inverse[0],
            point_slice,
            label_chunk[8:, :256],
            label_chunk[8:, 256:],
            coeff_chunk[8:],
        ],
        0,
    )

    part = dot(columns(coeffs[1]), diag_inverse[1], 1, 1)
    part, off_block = lax.optimization_barrier((part, off_block))
    off_other = swap(off_block, "h")
    part = scatter_sum(part.reshape(8, 32, 128), xc).reshape(2, 16, 128)
    keep = lax.dynamic_index_in_dim(part, h, 0, keepdims=False)
    send = lax.dynamic_index_in_dim(part, 1 - h, 0, keepdims=False)
    send, pack = lax.optimization_barrier((send, pack))
    part = keep + swap(send, "h")
    pack = swap(pack, "h")
    second = gather(part, xc, 8).reshape(128, 128)

    carried = dot(second, jnp.concatenate([off_block, off_other], 0), 1, 1)
    carried = scatter_sum(carried.reshape(16, 8, 512), zy)
    carried = carried + swap(carried, "w")
    rest = jnp.concatenate([coeff_chunk[:8], pack[176:]], 1) - carried
    rest = gather(rest, zy, 16).reshape(128, 512)

    diag = jnp.concatenate([diag_inverse[0], pack[:128]], 1)
    first = dot(rest, diag, 1, 1)
    first, point_slice = lax.optimization_barrier((first, pack[128:160]))
    points_other = gather(point_slice, zy, 16).reshape(512, 256)
    first = first + swap(first, "c")
    first = first + swap(first, "v")
    first = first + swap(first, "u")
    first, points_other = lax.optimization_barrier((first, points_other))
    solved = jnp.concatenate([first, second], 1)

    flat = centres.reshape(256, 256)

    def kernel_tile(rows):
        score = dot(rows, flat, 1, 1) / math.sqrt(rows.shape[1])
        return score + score * score * score / 3.0

    kernel = jnp.concatenate([kernel_tile(points), kernel_tile(points_other)], 0)
    pred_scale = 1.0 / (2.0 * math.sqrt(256 * 32))
    pred = scatter_sum(dot(solved, kernel, 1, 1).reshape(16, 8, 1024), zy)
    pred = pred + swap(pred, "w")
    target = jnp.concatenate([label_chunk[:8], pack[160:168], pack[168:176]], 1)
    weights = gather(jnp.tanh(pred * pred_scale - target), zy, 16).reshape(128, 1024)

    scale = 1.0 / (2.0 * math.sqrt(points.shape[0] * 16))
    term = dot(weights, kernel, 1, 0)
    term = scatter_sum(term.reshape(8, 16, 256), xc) * scale
    return term.reshape(16, 2, 128).transpose(1, 2, 0)


def solution(mesh):
    fine = Mesh(mesh.devices.reshape(tuple(SIZES.values())), tuple(SIZES))
    return jax.shard_map(
        local,
        mesh=fine,
        in_specs=(
            P(PTS, None),
            P(PTS, None),
            P(None, CTR, None),
            P(None, PTS, None),
            P(None, CTR, PTS),
            P(PTS, CTR),
        ),
        out_specs=P(None, CTR, PTS),
        check_vma=False,
    )
```

```python
import math

import jax
import jax.numpy as jnp
from jax import lax
from jax.sharding import Mesh
from jax.sharding import PartitionSpec as P

PTS = ("x", "h", "c")
CTR = ("w", "z", "y")
SIZES = {"x": 4, "h": 2, "c": 2, "w": 2, "z": 4, "y": 4}
HIGH = lax.Precision.HIGH


def dot(a, b, ca, cb):
    return lax.dot_general(
        a, b, (((ca,), (cb,)), ((), ())), precision=HIGH, preferred_element_type=jnp.float32
    )


def swap(a, axis):
    return lax.ppermute(a, axis, [(0, 1), (1, 0)])


def exchange(a, axes):
    return lax.all_to_all(a, axes, 0, 0, tiled=True)


def copies(a, n):
    return jnp.broadcast_to(a[None], (n, *a.shape))


def local(points, labels, centres, coeffs, diag_inverse, off_block):
    zy, xy = ("z", "y"), ("x", "y")
    y, z = lax.axis_index("y"), lax.axis_index("z")

    part = dot(coeffs[1], diag_inverse[1], 0, 1)
    part = jnp.sum(exchange(part.reshape(4, 64, 128), "x"), 0)

    diag = diag_inverse[0].reshape(128, 2, 128).transpose(1, 0, 2).reshape(256, 128)
    coeff = coeffs[0].T.reshape(4, 64, 2, 128).transpose(0, 2, 1, 3).reshape(4, 128, 128)
    own = jnp.concatenate([copies(off_block, 4), copies(diag, 4), coeff], 1)
    part, own = lax.optimization_barrier((part, own))
    blocks = exchange(own, "x")
    part = part + swap(part, "c")
    part = part + swap(part, "h")
    second, blocks = lax.optimization_barrier((part, blocks))

    carried = dot(second, blocks[:, :256], 1, 2)
    carried = carried.reshape(4, 16, 4, 256).transpose(0, 2, 1, 3).reshape(16, 16, 256)
    carried = jnp.sum(exchange(carried, zy), 0)
    coeff = blocks[:, 512:].reshape(4, 2, 64, 128)
    coeff = lax.dynamic_slice(coeff, (y, 0, z * 16, 0), (1, 2, 16, 128))
    coeff = coeff.reshape(2, 16, 128).transpose(1, 0, 2).reshape(16, 256)
    rest = (coeff - carried) - swap(carried, "w")
    rest, centres = lax.optimization_barrier((rest, centres))
    centre_copies = copies(centres.reshape(256, 256), 4)
    rest = exchange(copies(rest, 16), zy)
    rest = rest.reshape(4, 4, 16, 2, 128).transpose(0, 2, 1, 3, 4).reshape(64, 8, 128)

    diag = blocks[:, 256:512].reshape(8, 128, 128)
    first = lax.dot_general(
        rest,
        diag,
        (((1, 2), (0, 2)), ((), ())),
        precision=HIGH,
        preferred_element_type=jnp.float32,
    )
    first, centre_copies = lax.optimization_barrier((first, centre_copies))
    centres_y = exchange(centre_copies, "y").reshape(1024, 256)
    first = first + swap(first, "c")
    first = first + swap(first, "h")
    first, centres_y = lax.optimization_barrier((first, centres_y))

    solved = jnp.concatenate([first, second], 1).reshape(4, 16, 256)
    solved = exchange(copies(solved, 4).reshape(16, 16, 256), xy)
    solved = solved.reshape(4, 4, 16, 256).transpose(0, 2, 1, 3).reshape(64, 1024)

    score = dot(points, centres_y, 1, 1) / math.sqrt(points.shape[1])
    kernel = score + score * score * score / 3.0
    pred_scale = 1.0 / (2.0 * math.sqrt(256 * 32))
    pred = dot(solved, kernel, 1, 1).reshape(4, 16, 512)
    pred = jnp.sum(exchange(pred, "z"), 0)
    pred = pred + swap(pred, "w")

    row = lax.broadcasted_iota(jnp.int32, (16, 256), 0)
    chosen = lax.broadcasted_iota(jnp.int32, (16, 256), 1) == z * 64 + y * 16 + row
    target = lax.dot_general(
        chosen.astype(labels.dtype),
        labels,
        (((1,), (1,)), ((), ())),
        preferred_element_type=jnp.float32,
    )
    weights = jnp.tanh(pred * pred_scale - target)
    weights = exchange(copies(weights, 4), "z").reshape(64, 512)

    scale = 1.0 / (2.0 * math.sqrt(points.shape[0] * 16))
    term = dot(weights, kernel, 1, 0)
    term = term.reshape(4, 16, 4, 256).transpose(0, 2, 1, 3).reshape(16, 16, 256)
    term = jnp.sum(exchange(term, xy).reshape(4, 4, 16, 256), 0)
    term = jnp.sum(exchange(term, ("h", "c")), 0) * scale
    return term.reshape(16, 2, 128).transpose(1, 2, 0)


def solution(mesh):
    fine = Mesh(mesh.devices.reshape(tuple(SIZES.values())), tuple(SIZES))
    return jax.shard_map(
        local,
        mesh=fine,
        in_specs=(
            P(PTS, None),
            P(PTS, None),
            P(None, CTR, None),
            P(None, PTS, None),
            P(None, CTR, PTS),
            P(PTS, CTR),
        ),
        out_specs=P(None, CTR, PTS),
        check_vma=False,
    )
```

```python
import math

import jax
import jax.numpy as jnp
from jax import lax
from jax.sharding import Mesh
from jax.sharding import PartitionSpec as P

PTS = ("x", "h", "c")
CTR = ("w", "z", "y")
SIZES = {"x": 4, "h": 2, "c": 2, "w": 2, "z": 4, "y": 4}
HIGH = lax.Precision.HIGH


def dot(a, b, ca, cb):
    return lax.dot_general(
        a, b, (((ca,), (cb,)), ((), ())), precision=HIGH, preferred_element_type=jnp.float32
    )


def halves(a):
    high = lax.reduce_precision(a, 8, 7)
    return high.astype(jnp.bfloat16), (a - high).astype(jnp.bfloat16)


def dot_halves(a, b, ca, cb, free):
    high, low = halves(a)

    def one(left, right):
        return lax.dot_general(
            left, right, ((ca, cb), ((), ())), preferred_element_type=jnp.float32
        )

    both = one(jnp.concatenate([high, low], free), b[0])
    rows = a.shape[free]
    return both[:rows] + (both[rows:] + one(high, b[1]))


def swap(a, axis):
    return lax.ppermute(a, axis, [(0, 1), (1, 0)])


def exchange(a, axes):
    return lax.all_to_all(a, axes, 0, 0, tiled=True)


def copies(a, n):
    return jnp.broadcast_to(a[None], (n, *a.shape))


def local(points, labels, centres, coeffs, diag_inverse, off_block):
    zy, yx = ("z", "y"), ("y", "x")
    y, z = lax.axis_index("y"), lax.axis_index("z")

    part = dot(coeffs[1], diag_inverse[1], 0, 1)
    part = jnp.sum(exchange(part.reshape(4, 64, 128), "x"), 0)

    diag = diag_inverse[0].reshape(128, 2, 128).transpose(1, 0, 2).reshape(256, 128)
    coeff = coeffs[0].T.reshape(4, 64, 2, 128).transpose(0, 2, 1, 3).reshape(4, 128, 128)
    own = jnp.concatenate([copies(off_block, 4), copies(diag, 4), coeff], 1)
    centre_copies = copies(centres.reshape(256, 256), 4)
    part, own, centre_copies = lax.optimization_barrier((part, own, centre_copies))
    blocks = exchange(own, "x")
    part = part + swap(part, "c")
    part = part + swap(part, "h")
    second, blocks = lax.optimization_barrier((part, blocks))

    carried = dot(second, blocks[:, :256], 1, 2).transpose(1, 0, 2)
    carried = jnp.sum(exchange(carried.reshape(16, 16, 256), zy), 0)
    coeff = blocks[:, 512:].reshape(4, 2, 64, 128)
    coeff = lax.dynamic_slice(coeff, (z, 0, y * 16, 0), (1, 2, 16, 128))
    coeff = coeff.reshape(2, 16, 128).transpose(1, 0, 2).reshape(16, 256)
    rest = (coeff - carried) - swap(carried, "w")
    rest = exchange(copies(rest, 16), zy).reshape(4, 64, 256)

    def solve(side):
        return lax.dot_general(
            rest[:, :, side * 128 : side * 128 + 128],
            blocks[:, 256 + side * 128 : 384 + side * 128],
            (((0, 2), (0, 2)), ((), ())),
            precision=HIGH,
            preferred_element_type=jnp.float32,
        )

    first = solve(0) + solve(1)
    first, centre_copies = lax.optimization_barrier((first, centre_copies))
    centres_y = exchange(centre_copies, "y").reshape(1024, 256)
    first = first + swap(first, "c")
    first = first + swap(first, "h")
    first, centres_y = lax.optimization_barrier((first, centres_y))

    solved = jnp.concatenate([first, second], 1).reshape(4, 1, 16, 256)
    solved = jnp.broadcast_to(solved, (4, 4, 16, 256)).reshape(16, 16, 256)
    solved = exchange(solved, yx).reshape(4, 64, 256)

    score = dot(points, centres_y, 1, 1) / math.sqrt(points.shape[1])
    kernel = lax.optimization_barrier(halves(score + score * score * score / 3.0))
    pred_scale = 1.0 / (2.0 * math.sqrt(256 * 32))
    by_y = [side.reshape(512, 4, 256) for side in kernel]
    pred = dot_halves(solved, by_y, (0, 2), (1, 2), 1).reshape(4, 16, 512)
    pred = jnp.sum(exchange(pred, "z"), 0)
    pred = pred + swap(pred, "w")

    row = lax.broadcasted_iota(jnp.int32, (16, 256), 0)
    chosen = lax.broadcasted_iota(jnp.int32, (16, 256), 1) == z * 64 + y * 16 + row
    target = lax.dot_general(
        chosen.astype(labels.dtype),
        labels,
        (((1,), (1,)), ((), ())),
        preferred_element_type=jnp.float32,
    )
    weights = jnp.tanh(pred * pred_scale - target)
    weights = exchange(copies(weights, 4), "z").reshape(64, 512)

    scale = 1.0 / (2.0 * math.sqrt(points.shape[0] * 16))
    term = dot_halves(weights, kernel, (1,), (0,), 0)
    term = term.reshape(64, 4, 256).transpose(1, 0, 2).reshape(16, 16, 256)
    term = jnp.sum(exchange(term, yx).reshape(4, 4, 16, 256), 1)
    c, h = lax.axis_index("c"), lax.axis_index("h")
    term = term.reshape(2, 2, 16, 256)
    keep = lax.dynamic_index_in_dim(term, c, 1, keepdims=False)
    send = lax.dynamic_index_in_dim(term, 1 - c, 1, keepdims=False)
    term = keep + swap(send, "c")
    keep = lax.dynamic_index_in_dim(term, h, 0, keepdims=False)
    send = lax.dynamic_index_in_dim(term, 1 - h, 0, keepdims=False)
    term = (keep + swap(send, "h")) * scale
    return term.reshape(16, 2, 128).transpose(1, 2, 0)


def solution(mesh):
    fine = Mesh(mesh.devices.reshape(tuple(SIZES.values())), tuple(SIZES))
    return jax.shard_map(
        local,
        mesh=fine,
        in_specs=(
            P(PTS, None),
            P(PTS, None),
            P(None, CTR, None),
            P(None, PTS, None),
            P(None, CTR, PTS),
            P(PTS, CTR),
        ),
        out_specs=P(None, CTR, PTS),
        check_vma=False,
    )
```

```python
import math

import jax
import jax.numpy as jnp
from jax import lax
from jax.sharding import Mesh
from jax.sharding import PartitionSpec as P

PTS = ("x", "h", "c")
CTR = ("w", "z", "y")
SIZES = {"x": 4, "h": 2, "c": 2, "w": 2, "z": 4, "y": 4}
HIGH = lax.Precision.HIGH


def dot(a, b, ca, cb):
    return lax.dot_general(
        a, b, (((ca,), (cb,)), ((), ())), precision=HIGH, preferred_element_type=jnp.float32
    )


def halves(a):
    high = lax.reduce_precision(a, 8, 7)
    return high.astype(jnp.bfloat16), (a - high).astype(jnp.bfloat16)


def dot_halves(a, b, ca, cb, free):
    high, low = halves(a)

    def one(left, right):
        return lax.dot_general(
            left, right, ((ca, cb), ((), ())), preferred_element_type=jnp.float32
        )

    both = one(jnp.concatenate([high, low], free), b[0])
    rows = a.shape[free]
    return both[:rows] + (both[rows:] + one(high, b[1]))


def swap(a, axis):
    return lax.ppermute(a, axis, [(0, 1), (1, 0)])


def exchange(a, axes):
    return lax.all_to_all(a, axes, 0, 0, tiled=True)


def copies(a, n):
    return jnp.broadcast_to(a[None], (n, *a.shape))


def local(points, labels, centres, coeffs, diag_inverse, off_block):
    zy, yx = ("z", "y"), ("y", "x")
    y, z = lax.axis_index("y"), lax.axis_index("z")

    part = dot(coeffs[1], diag_inverse[1], 0, 1)
    part = jnp.sum(exchange(part.reshape(4, 64, 128), "x"), 0)

    diag = diag_inverse[0].reshape(128, 2, 128).transpose(1, 0, 2).reshape(256, 128)
    coeff = coeffs[0].T.reshape(4, 64, 2, 128).transpose(0, 2, 1, 3).reshape(4, 128, 128)
    own = jnp.concatenate([copies(off_block, 4), copies(diag, 4), coeff], 1)
    part, own = lax.optimization_barrier((part, own))
    blocks = exchange(own, "x")
    part = part + swap(part, "c")
    part = part + swap(part, "h")
    second, blocks = lax.optimization_barrier((part, blocks))

    carried = dot(second, blocks[:, :256], 1, 2).transpose(1, 0, 2)
    carried, flat = lax.optimization_barrier((carried, centres.reshape(256, 256)))
    others = [flat] + [lax.ppermute(flat, "y", [(i, i ^ k) for i in range(4)]) for k in (1, 2, 3)]
    carried = jnp.sum(exchange(carried.reshape(16, 16, 256), zy), 0)
    coeff = blocks[:, 512:].reshape(4, 2, 64, 128)
    coeff = lax.dynamic_slice(coeff, (z, 0, y * 16, 0), (1, 2, 16, 128))
    coeff = coeff.reshape(2, 16, 128).transpose(1, 0, 2).reshape(16, 256)
    rest = (coeff - carried) - swap(carried, "w")
    rest = exchange(copies(rest, 16), zy).reshape(4, 64, 256)

    def solve(side):
        return lax.dot_general(
            rest[:, :, side * 128 : side * 128 + 128],
            blocks[:, 256 + side * 128 : 384 + side * 128],
            (((0, 2), (0, 2)), ((), ())),
            precision=HIGH,
            preferred_element_type=jnp.float32,
        )

    first = solve(0) + solve(1)
    first = first + swap(first, "c")
    first, others = lax.optimization_barrier((first, others))
    first = first + swap(first, "h")

    solved = jnp.concatenate([first, second], 1).reshape(4, 1, 16, 256)
    solved = jnp.broadcast_to(solved, (4, 4, 16, 256)).reshape(16, 16, 256)
    solved = exchange(solved, yx).reshape(4, 64, 256)

    others = jnp.stack(others)
    centres_y = [lax.dynamic_index_in_dim(others, y ^ k, 0, keepdims=False) for k in range(4)]
    score = dot(points, jnp.concatenate(centres_y, 0), 1, 1) / math.sqrt(points.shape[1])
    kernel = lax.optimization_barrier(halves(score + score * score * score / 3.0))
    pred_scale = 1.0 / (2.0 * math.sqrt(256 * 32))
    by_y = [side.reshape(512, 4, 256) for side in kernel]
    pred = dot_halves(solved, by_y, (0, 2), (1, 2), 1).reshape(4, 16, 512)
    pred = jnp.sum(exchange(pred, "z"), 0)
    pred = pred + swap(pred, "w")

    row = lax.broadcasted_iota(jnp.int32, (16, 256), 0)
    chosen = lax.broadcasted_iota(jnp.int32, (16, 256), 1) == z * 64 + y * 16 + row
    target = lax.dot_general(
        chosen.astype(labels.dtype),
        labels,
        (((1,), (1,)), ((), ())),
        preferred_element_type=jnp.float32,
    )
    weights = jnp.tanh(pred * pred_scale - target)
    weights = exchange(copies(weights, 4), "z").reshape(64, 512)

    scale = 1.0 / (2.0 * math.sqrt(points.shape[0] * 16))
    term = dot_halves(weights, kernel, (1,), (0,), 0)
    term = term.reshape(64, 4, 256).transpose(1, 0, 2).reshape(16, 16, 256)
    term = jnp.sum(exchange(term, yx).reshape(4, 4, 16, 256), 1)
    c, h = lax.axis_index("c"), lax.axis_index("h")
    term = term.reshape(2, 2, 16, 256)
    keep = lax.dynamic_index_in_dim(term, c, 1, keepdims=False)
    send = lax.dynamic_index_in_dim(term, 1 - c, 1, keepdims=False)
    term = keep + swap(send, "c")
    keep = lax.dynamic_index_in_dim(term, h, 0, keepdims=False)
    send = lax.dynamic_index_in_dim(term, 1 - h, 0, keepdims=False)
    term = (keep + swap(send, "h")) * scale
    return term.reshape(16, 2, 128).transpose(1, 2, 0)


def solution(mesh):
    fine = Mesh(mesh.devices.reshape(tuple(SIZES.values())), tuple(SIZES))
    return jax.shard_map(
        local,
        mesh=fine,
        in_specs=(
            P(PTS, None),
            P(PTS, None),
            P(None, CTR, None),
            P(None, PTS, None),
            P(None, CTR, PTS),
            P(PTS, CTR),
        ),
        out_specs=P(None, CTR, PTS),
        check_vma=False,
    )
```

```python
import math

import jax
import jax.numpy as jnp
from jax import lax
from jax.sharding import Mesh
from jax.sharding import PartitionSpec as P

PTS = ("x", "h", "c")
CTR = ("w", "z", "y")
SIZES = {"x": 4, "h": 2, "c": 2, "w": 2, "z": 4, "y": 4}
HIGH = lax.Precision.HIGH


def dot(a, b, ca, cb):
    return lax.dot_general(
        a, b, (((ca,), (cb,)), ((), ())), precision=HIGH, preferred_element_type=jnp.float32
    )


def halves(a):
    high = lax.reduce_precision(a, 8, 7)
    return high.astype(jnp.bfloat16), (a - high).astype(jnp.bfloat16)


def dot_halves(a, b, ca, cb, free):
    high, low = halves(a)

    def one(left, right):
        return lax.dot_general(
            left, right, ((ca, cb), ((), ())), preferred_element_type=jnp.float32
        )

    both = one(jnp.concatenate([high, low], free), b[0])
    rows = a.shape[free]
    return both[:rows] + (both[rows:] + one(high, b[1]))


def swap(a, axis):
    return lax.ppermute(a, axis, [(0, 1), (1, 0)])


def exchange(a, axes):
    return lax.all_to_all(a, axes, 0, 0, tiled=True)


def copies(a, n):
    return jnp.broadcast_to(a[None], (n, *a.shape))


def local(points, labels, centres, coeffs, diag_inverse, off_block):
    zy, yx = ("z", "y"), ("y", "x")
    y, z = lax.axis_index("y"), lax.axis_index("z")

    part = dot(coeffs[1], diag_inverse[1], 0, 1)
    part = jnp.sum(exchange(part.reshape(4, 64, 128), "x"), 0)

    diag = diag_inverse[0].reshape(128, 2, 128).transpose(1, 0, 2).reshape(256, 128)
    coeff = coeffs[0].T.reshape(4, 64, 2, 128).transpose(0, 2, 1, 3).reshape(4, 128, 128)
    own = jnp.concatenate([copies(off_block, 4), copies(diag, 4), coeff], 1)
    part, own = lax.optimization_barrier((part, own))
    blocks = exchange(own, "x")
    part = part + swap(part, "c")
    part = part + swap(part, "h")
    second, blocks = lax.optimization_barrier((part, blocks))

    carried = dot(second, blocks[:, :256], 1, 2).transpose(1, 0, 2)
    carried, flat = lax.optimization_barrier((carried, centres.reshape(256, 256)))
    others = [flat] + [lax.ppermute(flat, "y", [(i, i ^ k) for i in range(4)]) for k in (1, 2, 3)]
    carried = jnp.sum(exchange(carried.reshape(16, 16, 256), zy), 0)
    coeff = blocks[:, 512:].reshape(4, 2, 64, 128)
    coeff = lax.dynamic_slice(coeff, (z, 0, y * 16, 0), (1, 2, 16, 128))
    coeff = coeff.reshape(2, 16, 128).transpose(1, 0, 2).reshape(16, 256)
    rest = (coeff - carried) - swap(carried, "w")
    rest = exchange(copies(rest, 16), zy).reshape(4, 64, 256)

    def solve(side):
        return lax.dot_general(
            rest[:, :, side * 128 : side * 128 + 128],
            blocks[:, 256 + side * 128 : 384 + side * 128],
            (((0, 2), (0, 2)), ((), ())),
            precision=HIGH,
            preferred_element_type=jnp.float32,
        )

    first = solve(0) + solve(1)
    first = first + swap(first, "c")
    first = first + swap(first, "h")
    first, others = lax.optimization_barrier((first, others))

    solved = jnp.concatenate([first, second], 1).reshape(4, 1, 16, 256)
    solved = jnp.broadcast_to(solved, (4, 4, 16, 256)).reshape(16, 16, 256)
    solved = exchange(solved, yx).reshape(4, 64, 256)

    others = jnp.stack(others)
    centres_y = [lax.dynamic_index_in_dim(others, y ^ k, 0, keepdims=False) for k in range(4)]
    score = dot(points, jnp.concatenate(centres_y, 0), 1, 1) / math.sqrt(points.shape[1])
    kernel = lax.optimization_barrier(halves(score + score * score * score / 3.0))
    pred_scale = 1.0 / (2.0 * math.sqrt(256 * 32))
    by_y = [side.reshape(512, 4, 256) for side in kernel]
    pred = dot_halves(solved, by_y, (0, 2), (1, 2), 1).reshape(4, 16, 512)
    pred = jnp.sum(exchange(pred, "z"), 0)
    pred = pred + swap(pred, "w")

    row = lax.broadcasted_iota(jnp.int32, (16, 256), 0)
    chosen = lax.broadcasted_iota(jnp.int32, (16, 256), 1) == z * 64 + y * 16 + row
    target = lax.dot_general(
        chosen.astype(labels.dtype),
        labels,
        (((1,), (1,)), ((), ())),
        preferred_element_type=jnp.float32,
    )
    weights = jnp.tanh(pred * pred_scale - target)
    weights = exchange(copies(weights, 4), "z").reshape(64, 512)

    scale = 1.0 / (2.0 * math.sqrt(points.shape[0] * 16))
    term = dot_halves(weights, kernel, (1,), (0,), 0)
    term = term.reshape(64, 4, 256).transpose(1, 0, 2).reshape(16, 16, 256)
    term = jnp.sum(exchange(term, yx).reshape(4, 4, 16, 256), 1)
    c, h = lax.axis_index("c"), lax.axis_index("h")
    term = term.reshape(2, 2, 16, 256)
    keep = lax.dynamic_index_in_dim(term, c, 1, keepdims=False)
    send = lax.dynamic_index_in_dim(term, 1 - c, 1, keepdims=False)
    term = keep + swap(send, "c")
    keep = lax.dynamic_index_in_dim(term, h, 0, keepdims=False)
    send = lax.dynamic_index_in_dim(term, 1 - h, 0, keepdims=False)
    term = (keep + swap(send, "h")) * scale
    return term.reshape(16, 2, 128).transpose(1, 2, 0)


def solution(mesh):
    fine = Mesh(mesh.devices.reshape(tuple(SIZES.values())), tuple(SIZES))
    return jax.shard_map(
        local,
        mesh=fine,
        in_specs=(
            P(PTS, None),
            P(PTS, None),
            P(None, CTR, None),
            P(None, PTS, None),
            P(None, CTR, PTS),
            P(PTS, CTR),
        ),
        out_specs=P(None, CTR, PTS),
        check_vma=False,
    )
```

```python
import math

import jax
import jax.numpy as jnp
from jax import lax
from jax.sharding import Mesh
from jax.sharding import PartitionSpec as P

PTS = ("x", "h", "c")
CTR = ("w", "z", "y")
SIZES = {"x": 4, "h": 2, "c": 2, "w": 2, "z": 4, "y": 4}
HIGH = lax.Precision.HIGH


def dot(a, b, ca, cb):
    return lax.dot_general(
        a, b, (((ca,), (cb,)), ((), ())), precision=HIGH, preferred_element_type=jnp.float32
    )


def halves(a):
    high = lax.reduce_precision(a, 8, 7)
    return high.astype(jnp.bfloat16), (a - high).astype(jnp.bfloat16)


def dot_halves(a, b, ca, cb, free):
    high, low = halves(a)

    def one(left, right):
        return lax.dot_general(
            left, right, ((ca, cb), ((), ())), preferred_element_type=jnp.float32
        )

    both = one(jnp.concatenate([high, low], free), b[0])
    rows = a.shape[free]
    return both[:rows] + (both[rows:] + one(high, b[1]))


def swap(a, axis):
    return lax.ppermute(a, axis, [(0, 1), (1, 0)])


def exchange(a, axes):
    return lax.all_to_all(a, axes, 0, 0, tiled=True)


def copies(a, n):
    return jnp.broadcast_to(a[None], (n, *a.shape))


def local(points, labels, centres, coeffs, diag_inverse, off_block):
    zy, yx = ("z", "y"), ("y", "x")
    y, z = lax.axis_index("y"), lax.axis_index("z")

    part = dot(coeffs[1], diag_inverse[1], 0, 1)
    part = jnp.sum(exchange(part.reshape(4, 64, 128), "x"), 0)

    diag = diag_inverse[0].reshape(128, 2, 128).transpose(1, 0, 2).reshape(256, 128)
    coeff = coeffs[0].T.reshape(4, 64, 2, 128).transpose(0, 2, 1, 3).reshape(4, 128, 128)
    own = jnp.concatenate([copies(off_block, 4), copies(diag, 4), coeff], 1)
    part, own = lax.optimization_barrier((part, own))
    blocks = exchange(own, "x")
    part = part + swap(part, "c")
    part = part + swap(part, "h")
    second, blocks = lax.optimization_barrier((part, blocks))

    carried = dot(second, blocks[:, :256], 1, 2).transpose(1, 0, 2)
    carried, flat = lax.optimization_barrier((carried, centres.reshape(256, 256)))
    near, far, wrap = (lax.ppermute(flat, "y", [(i, i ^ k) for i in range(4)]) for k in (1, 2, 3))
    carried = jnp.sum(exchange(carried.reshape(16, 16, 256), zy), 0)
    coeff = blocks[:, 512:].reshape(4, 2, 64, 128)
    coeff = lax.dynamic_slice(coeff, (z, 0, y * 16, 0), (1, 2, 16, 128))
    coeff = coeff.reshape(2, 16, 128).transpose(1, 0, 2).reshape(16, 256)
    rest = (coeff - carried) - swap(carried, "w")
    rest, near, wrap = lax.optimization_barrier((rest, near, wrap))
    rest = exchange(copies(rest, 16), zy).reshape(4, 64, 256)

    def solve(side):
        return lax.dot_general(
            rest[:, :, side * 128 : side * 128 + 128],
            blocks[:, 256 + side * 128 : 384 + side * 128],
            (((0, 2), (0, 2)), ((), ())),
            precision=HIGH,
            preferred_element_type=jnp.float32,
        )

    first = solve(0) + solve(1)
    first = jnp.sum(exchange(copies(first, 4), ("h", "c")), 0)
    first, far = lax.optimization_barrier((first, far))

    solved = jnp.concatenate([first, second], 1).reshape(4, 1, 16, 256)
    solved = jnp.broadcast_to(solved, (4, 4, 16, 256)).reshape(16, 16, 256)
    solved = exchange(solved, yx).reshape(4, 64, 256)

    others = jnp.stack([flat, near, far, wrap])
    centres_y = [lax.dynamic_index_in_dim(others, y ^ k, 0, keepdims=False) for k in range(4)]
    score = dot(points, jnp.concatenate(centres_y, 0), 1, 1) / math.sqrt(points.shape[1])
    kernel = lax.optimization_barrier(halves(score + score * score * score / 3.0))
    pred_scale = 1.0 / (2.0 * math.sqrt(256 * 32))
    by_y = [side.reshape(512, 4, 256) for side in kernel]
    pred = dot_halves(solved, by_y, (0, 2), (1, 2), 1).reshape(4, 16, 512)
    pred = jnp.sum(exchange(pred, "z"), 0)
    pred = pred + swap(pred, "w")

    row = lax.broadcasted_iota(jnp.int32, (16, 256), 0)
    chosen = lax.broadcasted_iota(jnp.int32, (16, 256), 1) == z * 64 + y * 16 + row
    target = lax.dot_general(
        chosen.astype(labels.dtype),
        labels,
        (((1,), (1,)), ((), ())),
        preferred_element_type=jnp.float32,
    )
    weights = jnp.tanh(pred * pred_scale - target)
    weights = exchange(copies(weights, 4), "z").reshape(64, 512)

    scale = 1.0 / (2.0 * math.sqrt(points.shape[0] * 16))
    term = dot_halves(weights, kernel, (1,), (0,), 0)
    term = term.reshape(64, 4, 256).transpose(1, 0, 2).reshape(16, 16, 256)
    term = jnp.sum(exchange(term, yx).reshape(4, 4, 16, 256), 1)
    c, h = lax.axis_index("c"), lax.axis_index("h")
    term = term.reshape(2, 2, 16, 256)
    keep = lax.dynamic_index_in_dim(term, c, 1, keepdims=False)
    send = lax.dynamic_index_in_dim(term, 1 - c, 1, keepdims=False)
    term = keep + swap(send, "c")
    keep = lax.dynamic_index_in_dim(term, h, 0, keepdims=False)
    send = lax.dynamic_index_in_dim(term, 1 - h, 0, keepdims=False)
    term = (keep + swap(send, "h")) * scale
    return term.reshape(16, 2, 128).transpose(1, 2, 0)


def solution(mesh):
    fine = Mesh(mesh.devices.reshape(tuple(SIZES.values())), tuple(SIZES))
    return jax.shard_map(
        local,
        mesh=fine,
        in_specs=(
            P(PTS, None),
            P(PTS, None),
            P(None, CTR, None),
            P(None, PTS, None),
            P(None, CTR, PTS),
            P(PTS, CTR),
        ),
        out_specs=P(None, CTR, PTS),
        check_vma=False,
    )
```

```python
import math

import jax
import jax.numpy as jnp
from jax import lax
from jax.sharding import Mesh
from jax.sharding import PartitionSpec as P

PTS = ("x", "h", "c")
CTR = ("w", "z", "y")
SIZES = {"x": 4, "h": 2, "c": 2, "w": 2, "z": 4, "y": 4}
HIGH = lax.Precision.HIGH


def dot(a, b, ca, cb):
    return lax.dot_general(
        a, b, (((ca,), (cb,)), ((), ())), precision=HIGH, preferred_element_type=jnp.float32
    )


def halves(a):
    high = lax.reduce_precision(a, 8, 7)
    return high.astype(jnp.bfloat16), (a - high).astype(jnp.bfloat16)


def dot_halves(a, b, ca, cb, free):
    high, low = halves(a)

    def one(left, right):
        return lax.dot_general(
            left, right, ((ca, cb), ((), ())), preferred_element_type=jnp.float32
        )

    both = one(jnp.concatenate([high, low], free), b[0])
    rows = a.shape[free]
    return both[:rows] + (both[rows:] + one(high, b[1]))


def swap(a, axis):
    return lax.ppermute(a, axis, [(0, 1), (1, 0)])


def exchange(a, axes):
    return lax.all_to_all(a, axes, 0, 0, tiled=True)


def copies(a, n):
    return jnp.broadcast_to(a[None], (n, *a.shape))


def local(points, labels, centres, coeffs, diag_inverse, off_block):
    zy, yx = ("z", "y"), ("y", "x")
    y, z = lax.axis_index("y"), lax.axis_index("z")

    part = dot(coeffs[1], diag_inverse[1], 0, 1)
    part = jnp.sum(exchange(part.reshape(4, 64, 128), "x"), 0)

    diag = diag_inverse[0].reshape(128, 2, 128).transpose(1, 0, 2).reshape(256, 128)
    coeff = coeffs[0].T.reshape(4, 64, 2, 128).transpose(0, 2, 1, 3).reshape(4, 128, 128)
    own = jnp.concatenate([copies(off_block, 4), copies(diag, 4), coeff], 1)
    part, own = lax.optimization_barrier((part, own))
    blocks = exchange(own, "x")
    part = part + swap(part, "c")
    part = part + swap(part, "h")
    second, blocks = lax.optimization_barrier((part, blocks))

    carried = dot(second, blocks[:, :256], 1, 2).transpose(1, 0, 2)
    carried, flat = lax.optimization_barrier((carried, centres.reshape(256, 256)))
    near, far, wrap = (lax.ppermute(flat, "y", [(i, i ^ k) for i in range(4)]) for k in (1, 2, 3))
    carried = jnp.sum(exchange(carried.reshape(16, 16, 256), zy), 0)
    coeff = blocks[:, 512:].reshape(4, 2, 64, 128)
    coeff = lax.dynamic_slice(coeff, (z, 0, y * 16, 0), (1, 2, 16, 128))
    coeff = coeff.reshape(2, 16, 128).transpose(1, 0, 2).reshape(16, 256)
    rest = (coeff - carried) - swap(carried, "w")
    rest, near, wrap = lax.optimization_barrier((rest, near, wrap))
    rest = exchange(copies(rest, 16), zy).reshape(4, 64, 256)

    def solve(side):
        return lax.dot_general(
            rest[:, :, side * 128 : side * 128 + 128],
            blocks[:, 256 + side * 128 : 384 + side * 128],
            (((0, 2), (0, 2)), ((), ())),
            precision=HIGH,
            preferred_element_type=jnp.float32,
        )

    first = solve(0) + solve(1)
    first = first + swap(first, "c")
    first = first + swap(first, "h")
    first, far = lax.optimization_barrier((first, far))

    solved = jnp.concatenate([first, second], 1).reshape(4, 1, 16, 256)
    solved = jnp.broadcast_to(solved, (4, 4, 16, 256)).reshape(16, 16, 256)
    solved = exchange(solved, yx).reshape(4, 64, 256)

    others = jnp.stack([flat, near, far, wrap])
    centres_y = [lax.dynamic_index_in_dim(others, y ^ k, 0, keepdims=False) for k in range(4)]
    score = dot(points, jnp.concatenate(centres_y, 0), 1, 1) / math.sqrt(points.shape[1])
    kernel = lax.optimization_barrier(halves(score + score * score * score / 3.0))
    pred_scale = 1.0 / (2.0 * math.sqrt(256 * 32))
    by_y = [side.reshape(512, 4, 256) for side in kernel]
    pred = dot_halves(solved, by_y, (0, 2), (1, 2), 1).reshape(4, 16, 512)
    pred = jnp.sum(exchange(pred, "z"), 0)
    pred = pred + swap(pred, "w")

    row = lax.broadcasted_iota(jnp.int32, (16, 256), 0)
    chosen = lax.broadcasted_iota(jnp.int32, (16, 256), 1) == z * 64 + y * 16 + row
    target = lax.dot_general(
        chosen.astype(labels.dtype),
        labels,
        (((1,), (1,)), ((), ())),
        preferred_element_type=jnp.float32,
    )
    weights = jnp.tanh(pred * pred_scale - target)
    weights = exchange(copies(weights, 4), "z").reshape(64, 512)

    scale = 1.0 / (2.0 * math.sqrt(points.shape[0] * 16))
    term = dot_halves(weights, kernel, (1,), (0,), 0)
    term = term.reshape(64, 4, 256).transpose(1, 0, 2).reshape(16, 16, 256)
    term = jnp.sum(exchange(term, yx).reshape(4, 4, 16, 256), 1)
    c, h = lax.axis_index("c"), lax.axis_index("h")
    term = term.reshape(2, 2, 16, 256)
    keep = lax.dynamic_index_in_dim(term, c, 1, keepdims=False)
    send = lax.dynamic_index_in_dim(term, 1 - c, 1, keepdims=False)
    term = keep + swap(send, "c")
    keep = lax.dynamic_index_in_dim(term, h, 0, keepdims=False)
    send = lax.dynamic_index_in_dim(term, 1 - h, 0, keepdims=False)
    term = (keep + swap(send, "h")) * scale
    return term.reshape(16, 2, 128).transpose(1, 2, 0)


def solution(mesh):
    fine = Mesh(mesh.devices.reshape(tuple(SIZES.values())), tuple(SIZES))
    return jax.shard_map(
        local,
        mesh=fine,
        in_specs=(
            P(PTS, None),
            P(PTS, None),
            P(None, CTR, None),
            P(None, PTS, None),
            P(None, CTR, PTS),
            P(PTS, CTR),
        ),
        out_specs=P(None, CTR, PTS),
        check_vma=False,
    )
```

```python
import math

import jax
import jax.numpy as jnp
from jax import lax
from jax.sharding import Mesh
from jax.sharding import PartitionSpec as P

PTS = ("x", "h", "c")
CTR = ("w", "z", "y")
SIZES = {"x": 4, "h": 2, "c": 2, "w": 2, "z": 4, "y": 4}
HIGH = lax.Precision.HIGH


def dot(a, b, ca, cb):
    return lax.dot_general(
        a, b, (((ca,), (cb,)), ((), ())), precision=HIGH, preferred_element_type=jnp.float32
    )


def halves(a):
    high = lax.reduce_precision(a, 8, 7)
    return high.astype(jnp.bfloat16), (a - high).astype(jnp.bfloat16)


def dot_halves(a, b, ca, cb, free):
    high, low = halves(a)

    def one(left, right):
        return lax.dot_general(
            left, right, ((ca, cb), ((), ())), preferred_element_type=jnp.float32
        )

    both = one(jnp.concatenate([high, low], free), b[0])
    rows = a.shape[free]
    return both[:rows] + (both[rows:] + one(high, b[1]))


def swap(a, axis):
    return lax.ppermute(a, axis, [(0, 1), (1, 0)])


def exchange(a, axes):
    return lax.all_to_all(a, axes, 0, 0, tiled=True)


def copies(a, n):
    return jnp.broadcast_to(a[None], (n, *a.shape))


def local(points, labels, centres, coeffs, diag_inverse, off_block):
    zy, yx = ("z", "y"), ("y", "x")
    y, z = lax.axis_index("y"), lax.axis_index("z")

    row = lax.broadcasted_iota(jnp.int32, (16, 256), 0)
    chosen = lax.broadcasted_iota(jnp.int32, (16, 256), 1) == z * 64 + y * 16 + row
    target = lax.dot_general(
        chosen.astype(labels.dtype),
        labels,
        (((1,), (1,)), ((), ())),
        preferred_element_type=jnp.float32,
    )
    c0, h0 = lax.axis_index("c") == 0, lax.axis_index("h") == 0

    part = dot(coeffs[1], diag_inverse[1], 0, 1)
    part = jnp.sum(exchange(part.reshape(4, 64, 128), "x"), 0)

    diag = diag_inverse[0].reshape(128, 2, 128).transpose(1, 0, 2).reshape(256, 128)
    coeff = coeffs[0].T.reshape(4, 64, 2, 128).transpose(0, 2, 1, 3).reshape(4, 128, 128)
    own = jnp.concatenate([copies(off_block, 4), copies(diag, 4), coeff], 1)
    part, own = lax.optimization_barrier((part, own))
    blocks = exchange(own, "x")
    part = part + swap(part, "c")
    part = part + swap(part, "h")
    second, blocks = lax.optimization_barrier((part, blocks))

    carried = dot(second, blocks[:, :256], 1, 2).transpose(1, 0, 2)
    carried, flat = lax.optimization_barrier((carried, centres.reshape(256, 256)))
    near, far, wrap = (lax.ppermute(flat, "y", [(i, i ^ k) for i in range(4)]) for k in (1, 2, 3))
    carried = jnp.sum(exchange(carried.reshape(16, 16, 256), zy), 0)
    coeff = blocks[:, 512:].reshape(4, 2, 64, 128)
    coeff = lax.dynamic_slice(coeff, (z, 0, y * 16, 0), (1, 2, 16, 128))
    coeff = coeff.reshape(2, 16, 128).transpose(1, 0, 2).reshape(16, 256)
    rest = (coeff - carried) - swap(carried, "w")
    rest, near, wrap = lax.optimization_barrier((rest, near, wrap))
    rest = exchange(copies(rest, 16), zy).reshape(4, 64, 256)

    def solve(side):
        return lax.dot_general(
            rest[:, :, side * 128 : side * 128 + 128],
            blocks[:, 256 + side * 128 : 384 + side * 128],
            (((0, 2), (0, 2)), ((), ())),
            precision=HIGH,
            preferred_element_type=jnp.float32,
        )

    first = solve(0) + solve(1)
    first = first + swap(first, "c")
    first = first + swap(first, "h")
    first, far, target, c0, h0 = lax.optimization_barrier((first, far, target, c0, h0))

    solved = jnp.concatenate([first, second], 1).reshape(4, 1, 16, 256)
    solved = jnp.broadcast_to(solved, (4, 4, 16, 256)).reshape(16, 16, 256)
    solved = exchange(solved, yx).reshape(4, 64, 256)

    others = jnp.stack([flat, near, far, wrap])
    centres_y = [lax.dynamic_index_in_dim(others, y ^ k, 0, keepdims=False) for k in range(4)]
    score = dot(points, jnp.concatenate(centres_y, 0), 1, 1) / math.sqrt(points.shape[1])
    kernel = lax.optimization_barrier(halves(score + score * score * score / 3.0))
    pred_scale = 1.0 / (2.0 * math.sqrt(256 * 32))
    by_y = [side.reshape(512, 4, 256) for side in kernel]
    pred = dot_halves(solved, by_y, (0, 2), (1, 2), 1).reshape(4, 16, 512)
    pred = jnp.sum(exchange(pred, "z"), 0)
    pred = pred + swap(pred, "w")

    weights = jnp.tanh(pred * pred_scale - target)
    weights = exchange(copies(weights, 4), "z").reshape(64, 512)

    scale = 1.0 / (2.0 * math.sqrt(points.shape[0] * 16))
    term = dot_halves(weights, kernel, (1,), (0,), 0)
    term = term.reshape(64, 4, 256).transpose(1, 0, 2).reshape(16, 16, 256)
    term = jnp.sum(exchange(term, yx).reshape(4, 4, 16, 256), 1)
    term = term.reshape(2, 2, 16, 2, 128).transpose(0, 1, 3, 2, 4)
    term = jnp.where(c0, term[:, 0], term[:, 1]) + swap(jnp.where(c0, term[:, 1], term[:, 0]), "c")
    term = jnp.where(h0, term[0], term[1]) + swap(jnp.where(h0, term[1], term[0]), "h")
    return (term * scale).transpose(0, 2, 1)


def solution(mesh):
    fine = Mesh(mesh.devices.reshape(tuple(SIZES.values())), tuple(SIZES))
    return jax.shard_map(
        local,
        mesh=fine,
        in_specs=(
            P(PTS, None),
            P(PTS, None),
            P(None, CTR, None),
            P(None, PTS, None),
            P(None, CTR, PTS),
            P(PTS, CTR),
        ),
        out_specs=P(None, CTR, PTS),
        check_vma=False,
    )
```

```python
import math

import jax
import jax.numpy as jnp
from jax import lax
from jax.sharding import Mesh
from jax.sharding import PartitionSpec as P

PTS = ("x", "h", "c")
CTR = ("w", "z", "y")
SIZES = {"x": 4, "h": 2, "c": 2, "w": 2, "z": 4, "y": 4}
HIGH = lax.Precision.HIGH


def dot(a, b, ca, cb):
    return lax.dot_general(
        a, b, (((ca,), (cb,)), ((), ())), precision=HIGH, preferred_element_type=jnp.float32
    )


def halves(a):
    high = lax.reduce_precision(a, 8, 7)
    return high.astype(jnp.bfloat16), (a - high).astype(jnp.bfloat16)


def dot_halves(a, b, ca, cb, free):
    high, low = halves(a)

    def one(left, right):
        return lax.dot_general(
            left, right, ((ca, cb), ((), ())), preferred_element_type=jnp.float32
        )

    both = one(jnp.concatenate([high, low], free), b[0])
    rows = a.shape[free]
    return both[:rows] + (both[rows:] + one(high, b[1]))


def swap(a, axis):
    return lax.ppermute(a, axis, [(0, 1), (1, 0)])


def exchange(a, axes):
    return lax.all_to_all(a, axes, 0, 0, tiled=True)


def copies(a, n):
    return jnp.broadcast_to(a[None], (n, *a.shape))


def local(points, labels, centres, coeffs, diag_inverse, off_block):
    zy, yx = ("z", "y"), ("y", "x")
    y, z = lax.axis_index("y"), lax.axis_index("z")

    row = lax.broadcasted_iota(jnp.int32, (16, 256), 0)
    chosen = lax.broadcasted_iota(jnp.int32, (16, 256), 1) == z * 64 + y * 16 + row
    target = lax.dot_general(
        chosen.astype(labels.dtype),
        labels,
        (((1,), (1,)), ((), ())),
        preferred_element_type=jnp.float32,
    )
    c0, h0 = lax.axis_index("c") == 0, lax.axis_index("h") == 0

    part = dot(coeffs[1], diag_inverse[1], 0, 1)
    part, coeffs = lax.optimization_barrier((part, coeffs))
    part = jnp.sum(exchange(part.reshape(4, 64, 128), "x"), 0)

    diag = diag_inverse[0].reshape(128, 2, 128).transpose(1, 0, 2).reshape(256, 128)
    coeff = coeffs[0].T.reshape(4, 64, 2, 128).transpose(0, 2, 1, 3).reshape(4, 128, 128)
    own = jnp.concatenate([copies(off_block, 4), copies(diag, 4), coeff], 1)
    part, own = lax.optimization_barrier((part, own))
    blocks = exchange(own, "x")
    part = part + swap(part, "c")
    part = part + swap(part, "h")
    second, blocks = lax.optimization_barrier((part, blocks))

    carried = dot(second, blocks[:, :256], 1, 2).transpose(1, 0, 2)
    carried, flat = lax.optimization_barrier((carried, centres.reshape(256, 256)))
    near, far, wrap = (lax.ppermute(flat, "y", [(i, i ^ k) for i in range(4)]) for k in (1, 2, 3))
    carried = jnp.sum(exchange(carried.reshape(16, 16, 256), zy), 0)
    coeff = blocks[:, 512:].reshape(4, 2, 64, 128)
    coeff = lax.dynamic_slice(coeff, (z, 0, y * 16, 0), (1, 2, 16, 128))
    coeff = coeff.reshape(2, 16, 128).transpose(1, 0, 2).reshape(16, 256)
    rest = (coeff - carried) - swap(carried, "w")
    rest, near, wrap = lax.optimization_barrier((rest, near, wrap))
    rest = exchange(copies(rest, 16), zy).reshape(4, 64, 256)

    def solve(side):
        return lax.dot_general(
            rest[:, :, side * 128 : side * 128 + 128],
            blocks[:, 256 + side * 128 : 384 + side * 128],
            (((0, 2), (0, 2)), ((), ())),
            precision=HIGH,
            preferred_element_type=jnp.float32,
        )

    first = solve(0) + solve(1)
    first = first + swap(first, "c")
    first, far = lax.optimization_barrier((first, far))
    others = jnp.stack([flat, near, far, wrap])
    centres_y = [lax.dynamic_index_in_dim(others, y ^ k, 0, keepdims=False) for k in range(4)]
    score = dot(points, jnp.concatenate(centres_y, 0), 1, 1) / math.sqrt(points.shape[1])
    kernel = halves(score + score * score * score / 3.0)
    first = first + swap(first, "h")
    first, kernel, target, c0, h0 = lax.optimization_barrier((first, kernel, target, c0, h0))

    solved = jnp.concatenate([first, second], 1).reshape(4, 1, 16, 256)
    solved = jnp.broadcast_to(solved, (4, 4, 16, 256)).reshape(16, 16, 256)
    solved = exchange(solved, yx).reshape(4, 64, 256)

    pred_scale = 1.0 / (2.0 * math.sqrt(256 * 32))
    by_y = [side.reshape(512, 4, 256) for side in kernel]
    pred = dot_halves(solved, by_y, (0, 2), (1, 2), 1).reshape(4, 16, 512)
    pred = jnp.sum(exchange(pred, "z"), 0)
    pred = pred + swap(pred, "w")

    weights = jnp.tanh(pred * pred_scale - target)
    weights = exchange(copies(weights, 4), "z").reshape(64, 512)

    scale = 1.0 / (2.0 * math.sqrt(points.shape[0] * 16))
    term = dot_halves(weights, kernel, (1,), (0,), 0)
    term = term.reshape(4, 16, 4, 2, 128).transpose(2, 0, 3, 1, 4).reshape(16, 2, 16, 128)
    term = jnp.sum(exchange(term, yx).reshape(4, 4, 2, 16, 128), 1)
    term = term.reshape(2, 2, 2, 16, 128)
    term = jnp.where(c0, term[:, 0], term[:, 1]) + swap(jnp.where(c0, term[:, 1], term[:, 0]), "c")
    term = jnp.where(h0, term[0], term[1]) + swap(jnp.where(h0, term[1], term[0]), "h")
    return (term * scale).transpose(0, 2, 1)


def solution(mesh):
    fine = Mesh(mesh.devices.reshape(tuple(SIZES.values())), tuple(SIZES))
    return jax.shard_map(
        local,
        mesh=fine,
        in_specs=(
            P(PTS, None),
            P(PTS, None),
            P(None, CTR, None),
            P(None, PTS, None),
            P(None, CTR, PTS),
            P(PTS, CTR),
        ),
        out_specs=P(None, CTR, PTS),
        check_vma=False,
    )
```

```python
import math

import jax
import jax.numpy as jnp
from jax import lax
from jax.sharding import Mesh
from jax.sharding import PartitionSpec as P

PTS = ("x", "h", "c")
CTR = ("w", "z", "y")
SIZES = {"x": 4, "h": 2, "c": 2, "w": 2, "z": 4, "y": 4}
HIGH = lax.Precision.HIGH


def dot(a, b, ca, cb):
    return lax.dot_general(
        a, b, (((ca,), (cb,)), ((), ())), precision=HIGH, preferred_element_type=jnp.float32
    )


def halves(a):
    high = lax.reduce_precision(a, 8, 7)
    return high.astype(jnp.bfloat16), (a - high).astype(jnp.bfloat16)


def dot_halves(a, b, ca, cb, free):
    high, low = halves(a)

    def one(left, right):
        return lax.dot_general(
            left, right, ((ca, cb), ((), ())), preferred_element_type=jnp.float32
        )

    both = one(jnp.concatenate([high, low], free), b[0])
    rows = a.shape[free]
    return both[:rows] + (both[rows:] + one(high, b[1]))


def swap(a, axis):
    return lax.ppermute(a, axis, [(0, 1), (1, 0)])


def exchange(a, axes):
    return lax.all_to_all(a, axes, 0, 0, tiled=True)


def copies(a, n):
    return jnp.broadcast_to(a[None], (n, *a.shape))


def local(points, labels, centres, coeffs, diag_inverse, off_block):
    zy, yx = ("z", "y"), ("y", "x")
    y, z = lax.axis_index("y"), lax.axis_index("z")

    row = lax.broadcasted_iota(jnp.int32, (16, 256), 0)
    chosen = lax.broadcasted_iota(jnp.int32, (16, 256), 1) == z * 64 + y * 16 + row
    target = lax.dot_general(
        chosen.astype(labels.dtype),
        labels,
        (((1,), (1,)), ((), ())),
        preferred_element_type=jnp.float32,
    )
    c0, h0 = lax.axis_index("c") == 0, lax.axis_index("h") == 0

    part = dot(diag_inverse[1], coeffs[1], 1, 0)
    part, coeffs = lax.optimization_barrier((part, coeffs))
    part = part.T
    part = jnp.sum(exchange(part.reshape(4, 64, 128), "x"), 0)

    diag = diag_inverse[0].reshape(128, 2, 128).transpose(1, 0, 2).reshape(256, 128)
    coeff = coeffs[0].T.reshape(4, 64, 2, 128).transpose(0, 2, 1, 3).reshape(4, 128, 128)
    own = jnp.concatenate([copies(off_block, 4), copies(diag, 4), coeff], 1)
    part, own = lax.optimization_barrier((part, own))
    blocks = exchange(own, "x")
    part = part + swap(part, "c")
    part = part + swap(part, "h")
    second, blocks = lax.optimization_barrier((part, blocks))

    carried = dot(second, blocks[:, :256], 1, 2).transpose(1, 0, 2)
    carried, flat = lax.optimization_barrier((carried, centres.reshape(256, 256)))
    near, far, wrap = (lax.ppermute(flat, "y", [(i, i ^ k) for i in range(4)]) for k in (1, 2, 3))
    carried = jnp.sum(exchange(carried.reshape(16, 16, 256), zy), 0)
    coeff = blocks[:, 512:].reshape(4, 2, 64, 128)
    coeff = lax.dynamic_slice(coeff, (z, 0, y * 16, 0), (1, 2, 16, 128))
    coeff = coeff.reshape(2, 16, 128).transpose(1, 0, 2).reshape(16, 256)
    rest = (coeff - carried) - swap(carried, "w")
    rest, near, wrap = lax.optimization_barrier((rest, near, wrap))
    rest = exchange(copies(rest, 16), zy).reshape(4, 64, 256)

    def solve(side):
        return lax.dot_general(
            rest[:, :, side * 128 : side * 128 + 128],
            blocks[:, 256 + side * 128 : 384 + side * 128],
            (((0, 2), (0, 2)), ((), ())),
            precision=HIGH,
            preferred_element_type=jnp.float32,
        )

    first = solve(0) + solve(1)
    first = first + swap(first, "c")
    first, far = lax.optimization_barrier((first, far))
    others = jnp.stack([flat, near, far, wrap])
    centres_y = [lax.dynamic_index_in_dim(others, y ^ k, 0, keepdims=False) for k in range(4)]
    score = dot(points, jnp.concatenate(centres_y, 0), 1, 1) / math.sqrt(points.shape[1])
    kernel = halves(score + score * score * score / 3.0)
    first = first + swap(first, "h")
    first, kernel, target, c0, h0 = lax.optimization_barrier((first, kernel, target, c0, h0))

    solved = jnp.concatenate([first, second], 1).reshape(4, 1, 16, 256)
    solved = jnp.broadcast_to(solved, (4, 4, 16, 256)).reshape(16, 16, 256)
    solved = exchange(solved, yx).reshape(4, 64, 256)

    pred_scale = 1.0 / (2.0 * math.sqrt(256 * 32))
    by_y = [side.reshape(512, 4, 256) for side in kernel]
    pred = dot_halves(solved, by_y, (0, 2), (1, 2), 1).reshape(4, 16, 512)
    pred = jnp.sum(exchange(pred, "z"), 0)
    pred = pred + swap(pred, "w")

    weights = jnp.tanh(pred * pred_scale - target)
    weights = exchange(copies(weights, 4), "z").reshape(64, 512)

    scale = 1.0 / (2.0 * math.sqrt(points.shape[0] * 16))
    term = dot_halves(weights, kernel, (1,), (0,), 0)
    term = term.reshape(4, 16, 4, 2, 128).transpose(2, 0, 3, 1, 4).reshape(16, 2, 16, 128)
    term = jnp.sum(exchange(term, yx).reshape(4, 4, 2, 16, 128), 1)
    term = term.reshape(2, 2, 2, 16, 128)
    term = jnp.where(c0, term[:, 0], term[:, 1]) + swap(jnp.where(c0, term[:, 1], term[:, 0]), "c")
    term = jnp.where(h0, term[0], term[1]) + swap(jnp.where(h0, term[1], term[0]), "h")
    return (term * scale).transpose(0, 2, 1)


def solution(mesh):
    fine = Mesh(mesh.devices.reshape(tuple(SIZES.values())), tuple(SIZES))
    return jax.shard_map(
        local,
        mesh=fine,
        in_specs=(
            P(PTS, None),
            P(PTS, None),
            P(None, CTR, None),
            P(None, PTS, None),
            P(None, CTR, PTS),
            P(PTS, CTR),
        ),
        out_specs=P(None, CTR, PTS),
        check_vma=False,
    )
```

```python
import math

import jax
import jax.numpy as jnp
from jax import lax
from jax.sharding import Mesh
from jax.sharding import PartitionSpec as P

PTS = ("x", "h", "c")
CTR = ("w", "z", "y")
SIZES = {"x": 4, "h": 2, "c": 2, "w": 2, "z": 4, "y": 4}
HIGH = lax.Precision.HIGH


def dot(a, b, ca, cb):
    return lax.dot_general(
        a, b, (((ca,), (cb,)), ((), ())), precision=HIGH, preferred_element_type=jnp.float32
    )


def halves(a):
    high = lax.reduce_precision(a, 8, 7)
    return high.astype(jnp.bfloat16), (a - high).astype(jnp.bfloat16)


def dot_halves(a, b, ca, cb, free):
    high, low = halves(a)

    def one(left, right):
        return lax.dot_general(
            left, right, ((ca, cb), ((), ())), preferred_element_type=jnp.float32
        )

    both = one(jnp.concatenate([high, low], free), b[0])
    rows = a.shape[free]
    return both[:rows] + (both[rows:] + one(high, b[1]))


def swap(a, axis):
    return lax.ppermute(a, axis, [(0, 1), (1, 0)])


def exchange(a, axes):
    return lax.all_to_all(a, axes, 0, 0, tiled=True)


def copies(a, n):
    return jnp.broadcast_to(a[None], (n, *a.shape))


def local(points, labels, centres, coeffs, diag_inverse, off_block):
    zy = ("z", "y")
    x, y, z = lax.axis_index("x"), lax.axis_index("y"), lax.axis_index("z")

    row = lax.broadcasted_iota(jnp.int32, (64, 256), 0)
    start = row // 16 * 64 + y * 16 + row % 16
    chosen = lax.broadcasted_iota(jnp.int32, (64, 256), 1) == start
    label = lax.dot_general(
        chosen.astype(labels.dtype),
        labels,
        (((1,), (1,)), ((), ())),
        preferred_element_type=jnp.float32,
    )
    label = label.reshape(4, 16, 4, 128).transpose(0, 2, 1, 3).reshape(4, 64, 128)
    c0, h0 = lax.axis_index("c") == 0, lax.axis_index("h") == 0

    part = dot(diag_inverse[1], coeffs[1], 1, 0)
    part, coeffs = lax.optimization_barrier((part, coeffs))
    part = part.T
    part = jnp.sum(exchange(part.reshape(4, 64, 128), "x"), 0)

    diag = diag_inverse[0].reshape(128, 2, 128).transpose(1, 0, 2).reshape(256, 128)
    coeff = coeffs[0].T.reshape(4, 64, 2, 128).transpose(0, 2, 1, 3).reshape(4, 128, 128)
    own = jnp.concatenate([copies(off_block, 4), copies(diag, 4), coeff, label], 1)
    part, own = lax.optimization_barrier((part, own))
    blocks = exchange(own, "x")
    part = part + swap(part, "c")
    part = part + swap(part, "h")
    second, blocks = lax.optimization_barrier((part, blocks))

    carried = dot(second, blocks[:, :256], 1, 2).transpose(1, 0, 2)
    carried, flat = lax.optimization_barrier((carried, points))
    near, far, wrap = (lax.ppermute(flat, "x", [(i, i ^ k) for i in range(4)]) for k in (1, 2, 3))
    target = lax.dynamic_index_in_dim(blocks[:, 640:], z, 0, keepdims=False)
    target = target.reshape(4, 16, 128).transpose(1, 0, 2).reshape(16, 512)
    carried = jnp.sum(exchange(carried.reshape(16, 16, 256), zy), 0)
    coeff = blocks[:, 512:640].reshape(4, 2, 64, 128)
    coeff = lax.dynamic_slice(coeff, (z, 0, y * 16, 0), (1, 2, 16, 128))
    coeff = coeff.reshape(2, 16, 128).transpose(1, 0, 2).reshape(16, 256)
    rest = (coeff - carried) - swap(carried, "w")
    rest, near, wrap = lax.optimization_barrier((rest, near, wrap))
    rest = exchange(copies(rest, 16), zy).reshape(4, 64, 256)

    def solve(side):
        return lax.dot_general(
            rest[:, :, side * 128 : side * 128 + 128],
            blocks[:, 256 + side * 128 : 384 + side * 128],
            (((0, 2), (0, 2)), ((), ())),
            precision=HIGH,
            preferred_element_type=jnp.float32,
        )

    first = solve(0) + solve(1)
    first = first + swap(first, "c")
    first, far = lax.optimization_barrier((first, far))
    others = jnp.stack([flat, near, far, wrap])
    points_x = [lax.dynamic_index_in_dim(others, x ^ k, 0, keepdims=False) for k in range(4)]
    score = dot(jnp.concatenate(points_x, 0), centres.reshape(256, 256), 1, 1)
    score = score / math.sqrt(points.shape[1])
    kernel = halves(score + score * score * score / 3.0)
    first = first + swap(first, "h")
    first, kernel, target, c0, h0 = lax.optimization_barrier((first, kernel, target, c0, h0))

    solved = jnp.concatenate([first, second], 1)
    pred_scale = 1.0 / (2.0 * math.sqrt(256 * 32))
    pred = dot_halves(solved, kernel, (1,), (1,), 0)
    pred = pred.reshape(64, 4, 512).transpose(1, 0, 2).reshape(16, 16, 512)
    pred = jnp.sum(exchange(pred, zy), 0)
    pred = pred + swap(pred, "w")

    weights = jnp.tanh(pred * pred_scale - target)
    weights = exchange(copies(weights, 16), zy).reshape(4, 64, 512)

    scale = 1.0 / (2.0 * math.sqrt(points.shape[0] * 16))
    by_x = [side.reshape(4, 512, 256) for side in kernel]
    term = dot_halves(weights, by_x, (0, 2), (0, 1), 1)
    term = term.reshape(2, 2, 16, 2, 128).transpose(0, 1, 3, 2, 4)
    term = jnp.where(c0, term[:, 0], term[:, 1]) + swap(jnp.where(c0, term[:, 1], term[:, 0]), "c")
    term = jnp.where(h0, term[0], term[1]) + swap(jnp.where(h0, term[1], term[0]), "h")
    return (term * scale).transpose(0, 2, 1)


def solution(mesh):
    fine = Mesh(mesh.devices.reshape(tuple(SIZES.values())), tuple(SIZES))
    return jax.shard_map(
        local,
        mesh=fine,
        in_specs=(
            P(PTS, None),
            P(PTS, None),
            P(None, CTR, None),
            P(None, PTS, None),
            P(None, CTR, PTS),
            P(PTS, CTR),
        ),
        out_specs=P(None, CTR, PTS),
        check_vma=False,
    )
```

```python
import math

import jax
import jax.numpy as jnp
from jax import lax
from jax.sharding import Mesh
from jax.sharding import PartitionSpec as P

PTS = ("x", "h", "c")
CTR = ("w", "z", "y")
SIZES = {"x": 4, "h": 2, "c": 2, "w": 2, "z": 4, "y": 4}
HIGH = lax.Precision.HIGH


def dot(a, b, ca, cb):
    return lax.dot_general(
        a, b, (((ca,), (cb,)), ((), ())), precision=HIGH, preferred_element_type=jnp.float32
    )


def halves(a):
    high = lax.reduce_precision(a, 8, 7)
    return high.astype(jnp.bfloat16), (a - high).astype(jnp.bfloat16)


def dot_halves(a, b, ca, cb, free):
    high, low = halves(a)

    def one(left, right):
        return lax.dot_general(
            left, right, ((ca, cb), ((), ())), preferred_element_type=jnp.float32
        )

    both = one(jnp.concatenate([high, low], free), b[0])
    rows = a.shape[free]
    return both[:rows] + (both[rows:] + one(high, b[1]))


def swap(a, axis):
    return lax.ppermute(a, axis, [(0, 1), (1, 0)])


def exchange(a, axes):
    return lax.all_to_all(a, axes, 0, 0, tiled=True)


def copies(a, n):
    return jnp.broadcast_to(a[None], (n, *a.shape))


def local(points, labels, centres, coeffs, diag_inverse, off_block):
    zy = ("z", "y")
    x, y, z = lax.axis_index("x"), lax.axis_index("y"), lax.axis_index("z")

    row = lax.broadcasted_iota(jnp.int32, (64, 256), 0)
    start = row // 16 * 64 + y * 16 + row % 16
    chosen = lax.broadcasted_iota(jnp.int32, (64, 256), 1) == start
    label = lax.dot_general(
        chosen.astype(labels.dtype),
        labels,
        (((1,), (1,)), ((), ())),
        preferred_element_type=jnp.float32,
    )
    label = label.reshape(4, 16, 4, 128).transpose(0, 2, 1, 3).reshape(4, 64, 128)
    c0, h0 = lax.axis_index("c") == 0, lax.axis_index("h") == 0

    part = dot(diag_inverse[1], coeffs[1], 1, 0)
    part, coeffs = lax.optimization_barrier((part, coeffs))
    part = part.T
    part = jnp.sum(exchange(part.reshape(4, 64, 128), "x"), 0)

    diag = diag_inverse[0].reshape(128, 2, 128).transpose(1, 0, 2).reshape(256, 128)
    coeff = coeffs[0].T.reshape(4, 64, 2, 128).transpose(0, 2, 1, 3).reshape(4, 128, 128)
    own = jnp.concatenate([copies(off_block, 4), copies(diag, 4), coeff, label], 1)
    part, own = lax.optimization_barrier((part, own))
    blocks = exchange(own, "x")
    part = part + swap(part, "c")
    part = part + swap(part, "h")
    second, blocks = lax.optimization_barrier((part, blocks))

    carried = dot(second, blocks[:, :256], 1, 2).transpose(1, 0, 2)
    carried, flat = lax.optimization_barrier((carried, points))
    near, far, wrap = (lax.ppermute(flat, "x", [(i, i ^ k) for i in range(4)]) for k in (1, 2, 3))
    carried = jnp.sum(exchange(carried.reshape(16, 16, 256), zy), 0)
    coeff = blocks[:, 512:640].reshape(4, 2, 64, 128)
    coeff = lax.dynamic_slice(coeff, (z, 0, y * 16, 0), (1, 2, 16, 128))
    coeff = coeff.reshape(2, 16, 128).transpose(1, 0, 2).reshape(16, 256)
    rest = (coeff - carried) - swap(carried, "w")
    rest, near, wrap = lax.optimization_barrier((rest, near, wrap))
    rest = exchange(copies(rest, 16), zy).reshape(4, 64, 256)

    def solve(side):
        return lax.dot_general(
            rest[:, :, side * 128 : side * 128 + 128],
            blocks[:, 256 + side * 128 : 384 + side * 128],
            (((0, 2), (0, 2)), ((), ())),
            precision=HIGH,
            preferred_element_type=jnp.float32,
        )

    first = solve(0) + solve(1)
    first = first + swap(first, "c")
    first, flat, near, wrap, blocks = lax.optimization_barrier((first, flat, near, wrap, blocks))
    target = lax.dynamic_slice(blocks, (z, 640, 0), (1, 64, 128))
    target = target.reshape(4, 16, 128).transpose(1, 0, 2).reshape(16, 512)
    others = jnp.stack([flat, near, far, wrap])
    points_x = [lax.dynamic_index_in_dim(others, x ^ k, 0, keepdims=False) for k in range(4)]
    score = dot(jnp.concatenate(points_x, 0), centres.reshape(256, 256), 1, 1)
    score = score / math.sqrt(points.shape[1])
    kernel = halves(score + score * score * score / 3.0)
    first = first + swap(first, "h")
    first, kernel, target, c0, h0 = lax.optimization_barrier((first, kernel, target, c0, h0))

    solved = jnp.concatenate([first, second], 1)
    pred_scale = 1.0 / (2.0 * math.sqrt(256 * 32))
    pred = dot_halves(solved, kernel, (1,), (1,), 0)
    pred = pred.reshape(64, 4, 512).transpose(1, 0, 2).reshape(16, 16, 512)
    pred = jnp.sum(exchange(pred, zy), 0)
    pred = pred + swap(pred, "w")

    weights = jnp.tanh(pred * pred_scale - target)
    weights = exchange(copies(weights, 16), zy).reshape(4, 64, 512)

    scale = 1.0 / (2.0 * math.sqrt(points.shape[0] * 16))
    by_x = [side.reshape(4, 512, 256) for side in kernel]
    term = dot_halves(weights, by_x, (0, 2), (0, 1), 1)
    term = term.reshape(2, 2, 16, 2, 128).transpose(0, 1, 3, 2, 4)
    term = jnp.where(c0, term[:, 0], term[:, 1]) + swap(jnp.where(c0, term[:, 1], term[:, 0]), "c")
    term = jnp.where(h0, term[0], term[1]) + swap(jnp.where(h0, term[1], term[0]), "h")
    return (term * scale).transpose(0, 2, 1)


def solution(mesh):
    fine = Mesh(mesh.devices.reshape(tuple(SIZES.values())), tuple(SIZES))
    return jax.shard_map(
        local,
        mesh=fine,
        in_specs=(
            P(PTS, None),
            P(PTS, None),
            P(None, CTR, None),
            P(None, PTS, None),
            P(None, CTR, PTS),
            P(PTS, CTR),
        ),
        out_specs=P(None, CTR, PTS),
        check_vma=False,
    )
```

```python
import math

import jax
import jax.numpy as jnp
from jax import lax
from jax.sharding import Mesh
from jax.sharding import PartitionSpec as P

PTS = ("x", "h", "c")
CTR = ("w", "z", "y")
SIZES = {"x": 4, "h": 2, "c": 2, "w": 2, "z": 4, "y": 4}
HIGH = lax.Precision.HIGH


def dot(a, b, ca, cb):
    return lax.dot_general(
        a, b, (((ca,), (cb,)), ((), ())), precision=HIGH, preferred_element_type=jnp.float32
    )


def halves(a):
    high = lax.reduce_precision(a, 8, 7)
    return high.astype(jnp.bfloat16), (a - high).astype(jnp.bfloat16)


def dot_halves(a, b, ca, cb, free):
    high, low = halves(a)

    def one(left, right):
        return lax.dot_general(
            left, right, ((ca, cb), ((), ())), preferred_element_type=jnp.float32
        )

    both = one(jnp.concatenate([high, low], free), b[0])
    rows = a.shape[free]
    return both[:rows] + (both[rows:] + one(high, b[1]))


def swap(a, axis):
    return lax.ppermute(a, axis, [(0, 1), (1, 0)])


def exchange(a, axes):
    return lax.all_to_all(a, axes, 0, 0, tiled=True)


def copies(a, n):
    return jnp.broadcast_to(a[None], (n, *a.shape))


def local(points, labels, centres, coeffs, diag_inverse, off_block):
    zy = ("z", "y")
    x, y, z = lax.axis_index("x"), lax.axis_index("y"), lax.axis_index("z")

    row = lax.broadcasted_iota(jnp.int32, (64, 256), 0)
    start = row // 16 * 64 + y * 16 + row % 16
    chosen = lax.broadcasted_iota(jnp.int32, (64, 256), 1) == start
    label = lax.dot_general(
        chosen.astype(labels.dtype),
        labels,
        (((1,), (1,)), ((), ())),
        preferred_element_type=jnp.float32,
    )
    label = label.reshape(4, 16, 4, 128).transpose(0, 2, 1, 3).reshape(4, 64, 128)
    c0, h0 = lax.axis_index("c") == 0, lax.axis_index("h") == 0

    part = dot(diag_inverse[1], coeffs[1], 1, 0)
    part, coeffs = lax.optimization_barrier((part, coeffs))
    part = part.T
    part = jnp.sum(exchange(part.reshape(4, 64, 128), "x"), 0)

    diag = diag_inverse[0].reshape(128, 2, 128).transpose(1, 0, 2).reshape(256, 128)
    coeff = coeffs[0].T.reshape(4, 64, 2, 128).transpose(0, 2, 1, 3).reshape(4, 128, 128)
    own = jnp.concatenate([copies(off_block, 4), copies(diag, 4), coeff, label], 1)
    part, own = lax.optimization_barrier((part, own))
    blocks = exchange(own, "x")
    part = part + swap(part, "c")
    part = part + swap(part, "h")
    second, blocks = lax.optimization_barrier((part, blocks))

    carried = dot(second, blocks[:, :256], 1, 2).transpose(1, 0, 2)
    carried, flat = lax.optimization_barrier((carried, points))
    near, far, wrap = (lax.ppermute(flat, "x", [(i, i ^ k) for i in range(4)]) for k in (1, 2, 3))
    target = lax.dynamic_index_in_dim(blocks[:, 640:], z, 0, keepdims=False)
    target = target.reshape(4, 16, 128).transpose(1, 0, 2).reshape(16, 512)
    carried = jnp.sum(exchange(carried.reshape(16, 16, 256), zy), 0)
    coeff = blocks[:, 512:640].reshape(4, 2, 64, 128)
    coeff = lax.dynamic_slice(coeff, (z, 0, y * 16, 0), (1, 2, 16, 128))
    coeff = coeff.reshape(2, 16, 128).transpose(1, 0, 2).reshape(16, 256)
    rest = (coeff - carried) - swap(carried, "w")
    rest, near, wrap = lax.optimization_barrier((rest, near, wrap))
    rest = exchange(copies(rest, 16), zy).reshape(4, 64, 256)

    def solve(side):
        return lax.dot_general(
            rest[:, :, side * 128 : side * 128 + 128],
            blocks[:, 256 + side * 128 : 384 + side * 128],
            (((0, 2), (0, 2)), ((), ())),
            precision=HIGH,
            preferred_element_type=jnp.float32,
        )

    first = solve(0) + solve(1)
    first = first + swap(first, "c")
    first, flat, near, wrap = lax.optimization_barrier((first, flat, near, wrap))
    others = jnp.stack([flat, near, far, wrap])
    points_x = [lax.dynamic_index_in_dim(others, x ^ k, 0, keepdims=False) for k in range(4)]
    score = dot(jnp.concatenate(points_x, 0), centres.reshape(256, 256), 1, 1)
    score = score / math.sqrt(points.shape[1])
    kernel = halves(score + score * score * score / 3.0)
    first = first + swap(first, "h")
    first, kernel, target, c0, h0 = lax.optimization_barrier((first, kernel, target, c0, h0))

    solved = jnp.concatenate([first, second], 1)
    pred_scale = 1.0 / (2.0 * math.sqrt(256 * 32))
    pred = dot_halves(solved, kernel, (1,), (1,), 0)
    pred = pred.reshape(64, 4, 512).transpose(1, 0, 2).reshape(16, 16, 512)
    pred = jnp.sum(exchange(pred, zy), 0)
    pred = pred + swap(pred, "w")

    weights = jnp.tanh(pred * pred_scale - target)
    weights = exchange(copies(weights, 16), zy).reshape(4, 64, 512)

    scale = 1.0 / (2.0 * math.sqrt(points.shape[0] * 16))
    by_x = [side.reshape(4, 512, 256) for side in kernel]
    term = dot_halves(weights, by_x, (0, 2), (0, 1), 1)
    term = term.reshape(2, 2, 16, 2, 128).transpose(0, 1, 3, 2, 4)
    term = jnp.where(c0, term[:, 0], term[:, 1]) + swap(jnp.where(c0, term[:, 1], term[:, 0]), "c")
    term = jnp.where(h0, term[0], term[1]) + swap(jnp.where(h0, term[1], term[0]), "h")
    return (term * scale).transpose(0, 2, 1)


def solution(mesh):
    fine = Mesh(mesh.devices.reshape(tuple(SIZES.values())), tuple(SIZES))
    return jax.shard_map(
        local,
        mesh=fine,
        in_specs=(
            P(PTS, None),
            P(PTS, None),
            P(None, CTR, None),
            P(None, PTS, None),
            P(None, CTR, PTS),
            P(PTS, CTR),
        ),
        out_specs=P(None, CTR, PTS),
        check_vma=False,
    )
```

```python
import math

import jax
import jax.numpy as jnp
from jax import lax
from jax.sharding import Mesh
from jax.sharding import PartitionSpec as P

PTS = ("x", "h", "c")
CTR = ("w", "z", "y")
SIZES = {"x": 4, "h": 2, "c": 2, "w": 2, "z": 4, "y": 4}
HIGH = lax.Precision.HIGH


def dot(a, b, ca, cb):
    return lax.dot_general(
        a, b, (((ca,), (cb,)), ((), ())), precision=HIGH, preferred_element_type=jnp.float32
    )


def halves(a):
    high = lax.reduce_precision(a, 8, 7)
    return high.astype(jnp.bfloat16), (a - high).astype(jnp.bfloat16)


def dot_halves(a, b, ca, cb, free):
    high, low = halves(a)

    def one(left, right):
        return lax.dot_general(
            left, right, ((ca, cb), ((), ())), preferred_element_type=jnp.float32
        )

    both = one(jnp.concatenate([high, low], free), b[0])
    rows = a.shape[free]
    return both[:rows] + (both[rows:] + one(high, b[1]))


def swap(a, axis):
    return lax.ppermute(a, axis, [(0, 1), (1, 0)])


def exchange(a, axes):
    return lax.all_to_all(a, axes, 0, 0, tiled=True)


def copies(a, n):
    return jnp.broadcast_to(a[None], (n, *a.shape))


def local(points, labels, centres, coeffs, diag_inverse, off_block):
    zy = ("z", "y")
    x, y, z = lax.axis_index("x"), lax.axis_index("y"), lax.axis_index("z")

    row = lax.broadcasted_iota(jnp.int32, (64, 256), 0)
    start = row // 16 * 64 + y * 16 + row % 16
    chosen = lax.broadcasted_iota(jnp.int32, (64, 256), 1) == start
    label = lax.dot_general(
        chosen.astype(labels.dtype),
        labels,
        (((1,), (1,)), ((), ())),
        preferred_element_type=jnp.float32,
    )
    label = label.reshape(4, 16, 4, 128).transpose(0, 2, 1, 3).reshape(4, 64, 128)
    c0, h0 = lax.axis_index("c") == 0, lax.axis_index("h") == 0

    part = dot(diag_inverse[1], coeffs[1], 1, 0)
    part, coeffs = lax.optimization_barrier((part, coeffs))
    part = part.T
    part = jnp.sum(exchange(part.reshape(4, 64, 128), "x"), 0)

    diag = diag_inverse[0].reshape(128, 2, 128).transpose(1, 0, 2).reshape(256, 128)
    coeff = coeffs[0].T.reshape(4, 64, 2, 128).transpose(0, 2, 1, 3).reshape(4, 128, 128)
    own = jnp.concatenate([copies(off_block, 4), copies(diag, 4), coeff, label], 1)
    part, own = lax.optimization_barrier((part, own))
    blocks = exchange(own, "x")
    part = part + swap(part, "c")
    part = part + swap(part, "h")
    second, blocks = lax.optimization_barrier((part, blocks))

    carried = dot(second, blocks[:, :256], 1, 2).transpose(1, 0, 2)
    carried, flat = lax.optimization_barrier((carried, points))
    near, far, wrap = (lax.ppermute(flat, "x", [(i, i ^ k) for i in range(4)]) for k in (1, 2, 3))
    target = lax.dynamic_index_in_dim(blocks[:, 640:], z, 0, keepdims=False)
    target = target.reshape(4, 16, 128).transpose(1, 0, 2).reshape(16, 512)
    carried = jnp.sum(exchange(carried.reshape(16, 16, 256), zy), 0)
    coeff = blocks[:, 512:640].reshape(4, 2, 64, 128)
    coeff = lax.dynamic_slice(coeff, (z, 0, y * 16, 0), (1, 2, 16, 128))
    coeff = coeff.reshape(2, 16, 128).transpose(1, 0, 2).reshape(16, 256)
    rest = (coeff - carried) - swap(carried, "w")
    rest, near, wrap, target = lax.optimization_barrier((rest, near, wrap, target))
    rest = exchange(copies(rest, 16), zy).reshape(4, 64, 256)

    def solve(side):
        return lax.dot_general(
            rest[:, :, side * 128 : side * 128 + 128],
            blocks[:, 256 + side * 128 : 384 + side * 128],
            (((0, 2), (0, 2)), ((), ())),
            precision=HIGH,
            preferred_element_type=jnp.float32,
        )

    first = solve(0) + solve(1)
    first = first + swap(first, "c")
    first, flat, near, wrap = lax.optimization_barrier((first, flat, near, wrap))
    others = jnp.stack([flat, near, far, wrap])
    points_x = [lax.dynamic_index_in_dim(others, x ^ k, 0, keepdims=False) for k in range(4)]
    score = dot(jnp.concatenate(points_x, 0), centres.reshape(256, 256), 1, 1)
    score = score / math.sqrt(points.shape[1])
    kernel = halves(score + score * score * score / 3.0)
    first = first + swap(first, "h")
    first, kernel, target, c0, h0 = lax.optimization_barrier((first, kernel, target, c0, h0))

    solved = jnp.concatenate([first, second], 1)
    pred_scale = 1.0 / (2.0 * math.sqrt(256 * 32))
    pred = dot_halves(solved, kernel, (1,), (1,), 0)
    pred = pred.reshape(64, 4, 512).transpose(1, 0, 2).reshape(16, 16, 512)
    pred = jnp.sum(exchange(pred, zy), 0)
    pred = pred + swap(pred, "w")

    weights = jnp.tanh(pred * pred_scale - target)
    weights = exchange(copies(weights, 16), zy).reshape(4, 64, 512)

    scale = 1.0 / (2.0 * math.sqrt(points.shape[0] * 16))
    by_x = [side.reshape(4, 512, 256) for side in kernel]
    term = dot_halves(weights, by_x, (0, 2), (0, 1), 1)
    term = term.reshape(2, 2, 16, 2, 128).transpose(0, 1, 3, 2, 4)
    term = jnp.where(c0, term[:, 0], term[:, 1]) + swap(jnp.where(c0, term[:, 1], term[:, 0]), "c")
    term = jnp.where(h0, term[0], term[1]) + swap(jnp.where(h0, term[1], term[0]), "h")
    return (term * scale).transpose(0, 2, 1)


def solution(mesh):
    fine = Mesh(mesh.devices.reshape(tuple(SIZES.values())), tuple(SIZES))
    return jax.shard_map(
        local,
        mesh=fine,
        in_specs=(
            P(PTS, None),
            P(PTS, None),
            P(None, CTR, None),
            P(None, PTS, None),
            P(None, CTR, PTS),
            P(PTS, CTR),
        ),
        out_specs=P(None, CTR, PTS),
        check_vma=False,
    )
```
